256 devices in a mesh: date: 16 (over z, y_hi), col: 16 (over x, y_lo, core).
Axes of the slice: x: 4, y: 4 (y_hi: 2, y_lo: 2; y = y_hi * 2 + y_lo), z: 8, core: 2. Of those that a mesh axis runs over, the one named last changes fastest.
Arguments:
- features: bfloat16 [16, 4, 32, 2048], P('date', None, None, 'col'), may hold values from -6 to 6
- column_map: int32 [16, 3, 3], P('date'), may hold values from -32768 to 32768, as said below
- pair_mask: int32 [16, 3], P('date'), may hold values 0 or 1
- disp_start: int32 [16], P('date'), may hold values from 0 to 32, as said below
Outputs:
- cost_volume: bfloat16 [16, 4, 8, 128, 2048], P('date', None, None, None, 'col')
The draws below stay inside these ranges and needn't reach their ends.
Inputs may be any that keep to these rules, and one draw needn't show every extreme that they name: column_map[d, o - 1] = (h0, h1, h2) with |h1| <= 2 and |h2| <= 128; h0 lies within the range and reaches both of its ends. `disp_start`: some date has first disparity 32.
All inputs are finite; a program needn't handle non-finite values. No bound on the sum of `pair_mask` on one device may be relied on, other than what follows from the above.
Results may differ from the reference program's by a relative error of at most 0.001.
Values may be sent and summed in bfloat16 or wider, within the bound.
A program may use at most 64 MiB of HBM per device.

```python
import jax
import jax.numpy as jnp
from jax import lax

CHANNELS = 32
GROUPS = 8
DISP = 128
DSTART = 32
SPAN = 8
SHIFTS = 3
ROWS = 4
DATES = 16
W = 2048


def draw_column_map(key, part):
    key_one, key_two, key_three, key_four, key_five = jax.random.split(key, 5)
    limit = SPAN * 4096
    shift_part = jax.random.randint(key_one, (DATES, SHIFTS), -limit, limit + 1)
    slope_part = jax.random.randint(key_two, (DATES, SHIFTS), -2, 3)
    row_part = jax.random.randint(key_three, (DATES, SHIFTS), -128, 129)
    total_pairs = DATES * SHIFTS
    top_at = jax.random.randint(key_four, (), 0, total_pairs)
    bottom_at = (top_at + 1 + jax.random.randint(key_five, (), 0, total_pairs - 1)) % total_pairs
    flat_ids = jnp.arange(total_pairs).reshape(DATES, SHIFTS)
    shift_part = jnp.where(flat_ids == top_at, limit, jnp.where(flat_ids == bottom_at, -limit, shift_part))
    return jnp.stack([shift_part, slope_part, row_part], axis=-1).astype(jnp.int32)


def draw_disp_start(key, part):
    key_one, key_two = jax.random.split(key, 2)
    picked = jax.random.randint(key_one, (DATES,), 0, DSTART + 1)
    top_at = jax.random.randint(key_two, (), 0, DATES)
    return jnp.where(jnp.arange(DATES) == top_at, DSTART, picked).astype(jnp.int32)


def touch_ends(result, stream_key, least, high):
    spot = [jax.random.randint(jax.random.fold_in(stream_key, axis), (), 0, length) for axis, length in enumerate(result.shape)]
    longest = result.shape.index(max(result.shape))
    beside = spot[:longest] + [(spot[longest] + 1) % result.shape[longest]] + spot[longest + 1:]
    return result.at[tuple(spot)].set(least).at[tuple(beside)].set(high)


def block_levels(stream_key, dims, cuts, least, top_value):
    def one(position, parts):
        draws = jax.random.uniform(jax.random.fold_in(jax.random.fold_in(stream_key, 6), position), (parts,), jnp.float32, least / len(cuts), top_value / len(cuts))
        return jnp.repeat(jnp.exp(draws), dims[position] // parts).reshape((-1,) + (1,) * (len(dims) - position - 1))

    gain = one(*cuts[0])
    for cut in cuts[1:]:
        gain = gain * one(*cut)
    return gain


def scatter_about(own_key, extent, deviation, most, shards=(), kind=jnp.bfloat16):
    loudness = block_levels(own_key, extent, shards, -0.22, 0.18) if shards else 1.0
    array = jax.random.normal(own_key, extent, jnp.float32) * deviation * loudness
    return jnp.minimum(jnp.maximum(array, -most), most).astype(kind)


def setup_inputs(seed: int = 0) -> dict:
    splits = jax.random.split(jax.random.key(seed), 5)
    return {
        "features": scatter_about(splits[0], (DATES, ROWS, CHANNELS, W), 1.0, 6.0, ((0, 16), (3, 16))),
        "column_map": draw_column_map(jax.random.fold_in(splits[4], 71), 0),
        "pair_mask": touch_ends((jax.random.randint(splits[2], (DATES, SHIFTS), 0, 4) < 3).astype(jnp.int32), jax.random.fold_in(splits[2], 1), 0, 1),
        "disp_start": draw_disp_start(jax.random.fold_in(splits[4], 71), 0),
    }


def resample(window, win_start, map_row, targets, mid_col):
    row_ids = jnp.arange(window.shape[0], dtype=jnp.int32)[:, None]
    numer = map_row[0] + map_row[1] * (targets[None, :] - mid_col) + map_row[2] * row_ids
    source = targets[None, :].astype(jnp.float32) + numer.astype(jnp.float32) / 4096.0
    lower = jnp.floor(source)
    weight = source - lower
    lower_index = lower.astype(jnp.int32) - win_start
    length = window.shape[2]

    def fetch_cols(index):
        inside = (index >= 0) & (index < length)
        clipped = jnp.clip(index, 0, length - 1)
        picked = jnp.take_along_axis(window, jnp.broadcast_to(clipped[:, None, :], (window.shape[0], window.shape[1], index.shape[1])), axis=2)
        return jnp.where(inside[:, None, :], picked.astype(jnp.float32), 0.0)

    return (1.0 - weight)[:, None, :] * fetch_cols(lower_index) + weight[:, None, :] * fetch_cols(lower_index + 1)


def correlate(ref_tile, warped):
    cols = ref_tile.shape[2]
    ref_float = ref_tile.astype(jnp.float32)

    def per_disp(disparity):
        shifted = lax.dynamic_slice_in_dim(warped, DISP - 1 - disparity, cols, axis=2)
        products = ref_float * shifted
        return products.reshape(ROWS, GROUPS, CHANNELS // GROUPS, cols).sum(axis=2)

    stacked = lax.map(per_disp, jnp.arange(DISP, dtype=jnp.int32))
    return jnp.transpose(stacked, (1, 2, 0, 3)) * (GROUPS / CHANNELS)


def reference(features, column_map, pair_mask, disp_start):
    def per_date(date):
        ref_tile = features[date]
        disp_first = disp_start[date]
        targets = jnp.arange(W + DISP - 1, dtype=jnp.int32) - disp_first - (DISP - 1)
        total = jnp.zeros((ROWS, GROUPS, DISP, W), jnp.float32)
        for step in range(1, SHIFTS + 1):
            partner = features[(date - step) % DATES]
            warped = resample(partner, 0, column_map[date, step - 1], targets, W // 2)
            total = total + pair_mask[date, step - 1].astype(jnp.float32) * correlate(ref_tile, warped)
        return total.astype(jnp.bfloat16)

    return lax.map(per_date, jnp.arange(DATES, dtype=jnp.int32))
```

```python
import functools

import jax
import jax.numpy as jnp
from jax import lax
from jax.experimental import pallas as pl
from jax.experimental.pallas import tpu as pltpu
from jax.sharding import PartitionSpec as P

GROUPS = 8
DISP = 128
SHIFTS = 3
LEFT2 = 48
RIGHT = 16
MESH = pl.DeviceIdType.MESH


def exchange_kernel(dates, col_count, tile_rows, map_ref, mask_ref, disp_ref, f_ref, w_ref,
                    own, win, winf, wt, dsend, drecv, csend, crecv):
    date = lax.axis_index("date")
    col = lax.axis_index("col")
    yc, cols = f_ref.shape
    rows = tile_rows
    chans = yc // rows
    at_left = LEFT2
    at_own = LEFT2 + cols
    at_right = LEFT2 + 2 * cols
    length = at_right + RIGHT

    def date_of(by):
        return lax.rem(date + by + dates, dates)

    def col_of(by):
        return lax.rem(col + by + col_count, col_count)

    barrier = pltpu.get_barrier_semaphore()
    for by in (-1, -2, -3):
        pl.semaphore_signal(barrier, inc=1, device_id={"date": date_of(by)}, device_id_type=MESH)
    for by in (-2, -1, 1):
        pl.semaphore_signal(barrier, inc=1, device_id={"col": col_of(by)}, device_id_type=MESH)
    eye = (lax.broadcasted_iota(jnp.int32, (cols, cols), 0)
           == lax.broadcasted_iota(jnp.int32, (cols, cols), 1)).astype(jnp.bfloat16)
    own[...] = lax.dot_general(eye, f_ref[...], (((1,), (1,)), ((), ())),
                               preferred_element_type=jnp.float32).astype(jnp.bfloat16)
    pl.semaphore_wait(barrier, 6)

    date_copies = []
    for o in range(SHIFTS):
        copy = pltpu.make_async_remote_copy(
            src_ref=own, dst_ref=win.at[o, pl.ds(at_own, cols)],
            send_sem=dsend.at[o], recv_sem=drecv.at[o],
            device_id={"date": date_of(o + 1)}, device_id_type=MESH)
        copy.start()
        date_copies.append(copy)

    col_copies = []
    for o in range(SHIFTS):
        date_copies[o].wait_recv()
        here = []
        for n, (src, size, dst, by) in enumerate((
                (at_own, cols, at_left, 1),
                (at_own + cols - LEFT2, LEFT2, 0, 2),
                (at_own, RIGHT, at_right, -1))):
            copy = pltpu.make_async_remote_copy(
                src_ref=win.at[o, pl.ds(src, size)], dst_ref=win.at[o, pl.ds(dst, size)],
                send_sem=csend.at[o, n], recv_sem=crecv.at[o, n],
                device_id={"col": col_of(by)}, device_id_type=MESH)
            copy.start()
            here.append(copy)
        col_copies.append(here)

    first_col = col * cols
    mid_col = cols * col_count // 2
    disp_first = disp_ref[0]
    start = first_col - disp_first - DISP
    span = cols + DISP
    row_ids = lax.broadcasted_iota(jnp.int32, (8, yc), 1) // chans
    sub_ids = lax.broadcasted_iota(jnp.int32, (8, yc), 0)
    for o in range(SHIFTS):
        for copy in col_copies[o]:
            copy.wait_recv()
        winf[o, :, :] = win[o].astype(jnp.float32)

        @pl.when(col == 0)
        def _():
            winf[o, :at_own, :] = jnp.zeros((at_own, yc), jnp.float32)

        @pl.when(col == 1)
        def _():
            winf[o, :at_left, :] = jnp.zeros((at_left, yc), jnp.float32)

        @pl.when(col == col_count - 1)
        def _():
            winf[o, at_right:, :] = jnp.zeros((RIGHT, yc), jnp.float32)

        h0, h1, h2 = map_ref[o, 0, 0], map_ref[o, 0, 1], map_ref[o, 0, 2]
        base = h0 + h1 * (start - mid_col)
        least = base + jnp.minimum(h1 * (span - 1), 0) + jnp.minimum(h2 * (rows - 1), 0)
        shift = least >> 12
        first_row = LEFT2 - disp_first + shift
        scale = mask_ref[0, o].astype(jnp.float32) * 0.25
        unit = scale / 4096.0
        numer = (base - shift * 4096) + h1 * sub_ids + h2 * row_ids
        ramp = numer.astype(jnp.float32) * unit
        step = (h1 * 8).astype(jnp.float32) * unit
        for i in range(span // 8):
            e = ramp + step * float(i) if i else ramp
            w0 = jnp.maximum(scale - e, 0.0)
            w2 = jnp.maximum(e - scale, 0.0)
            w1 = scale - w0 - w2
            part = (w0 * winf[o, pl.ds(first_row + 8 * i, 8), :]
                    + w1 * winf[o, pl.ds(first_row + 8 * i + 1, 8), :]
                    + w2 * winf[o, pl.ds(first_row + 8 * i + 2, 8), :])
            if o == 0:
                wt[pl.ds(8 * i, 8), :] = part
            else:
                wt[pl.ds(8 * i, 8), :] += part
    for n in range(span // cols):
        w_ref[:, pl.ds(n * cols, cols)] = wt[pl.ds(n * cols, cols), :].T
    for copy in date_copies:
        copy.wait_send()
    for here in col_copies:
        for copy in here:
            copy.wait_send()


def correlate_kernel(f_ref, w_ref, o_ref):
    groups, disps, cols = o_ref.shape[1:]
    chans = f_ref.shape[0] // groups
    lanes = lax.broadcasted_iota(jnp.int32, (8, cols), 1)
    for g in range(groups):
        lows, highs, refs = [], [], []
        for c in range(chans):
            row = g * chans + c
            wide = jnp.broadcast_to(w_ref[pl.ds(row, 1), :], (8, w_ref.shape[1]))
            skewed = pltpu.roll(wide, 0, 1, stride=1, stride_axis=0)
            lows.append(skewed[:, :cols])
            highs.append(skewed[:, cols:])
            refs.append(jnp.broadcast_to(f_ref[pl.ds(row, 1), :].astype(jnp.float32), (8, cols)))
        blocks = []
        for kb in range(disps // 8):
            total = None
            for c in range(chans):
                if kb == 0:
                    moved = highs[c]
                else:
                    moved = pltpu.roll(jnp.where(lanes >= cols - 8 * kb, lows[c], highs[c]), 8 * kb, 1)
                term = refs[c] * moved
                total = term if total is None else total + term
            blocks.append(total)
            if len(blocks) == 2:
                o_ref[0, g, pl.ds(8 * (kb - 1), 16), :] = jnp.concatenate(blocks, axis=0).astype(o_ref.dtype)
                blocks = []


def shards(features, column_map, pair_mask, disp_start):
    rows, chans, cols = features.shape[1:]
    yc = rows * chans
    tile = features.reshape(yc, cols)
    length = LEFT2 + 2 * cols + RIGHT
    dates, col_count = lax.axis_size("date"), lax.axis_size("col")
    smem = pl.BlockSpec(memory_space=pltpu.SMEM)
    vmem = pl.BlockSpec(memory_space=pltpu.VMEM)
    warped = pl.pallas_call(
        functools.partial(exchange_kernel, dates, col_count, rows),
        out_shape=jax.ShapeDtypeStruct((yc, cols + DISP), jnp.float32),
        in_specs=[smem, smem, smem, vmem],
        out_specs=vmem,
        scratch_shapes=[
            pltpu.VMEM((cols, yc), jnp.bfloat16),
            pltpu.VMEM((SHIFTS, length, yc), jnp.bfloat16),
            pltpu.VMEM((SHIFTS, length, yc), jnp.float32),
            pltpu.VMEM((cols + DISP, yc), jnp.float32),
            pltpu.SemaphoreType.DMA((SHIFTS,)),
            pltpu.SemaphoreType.DMA((SHIFTS,)),
            pltpu.SemaphoreType.DMA((SHIFTS, 3)),
            pltpu.SemaphoreType.DMA((SHIFTS, 3)),
        ],
        compiler_params=pltpu.CompilerParams(collective_id=0, has_side_effects=True),
        name="exchange",
    )(jnp.transpose(column_map, (1, 0, 2)), pair_mask, disp_start, tile)
    cost = pl.pallas_call(
        correlate_kernel,
        out_shape=jax.ShapeDtypeStruct((rows, GROUPS, DISP, cols), jnp.bfloat16),
        grid=(rows,),
        in_specs=[pl.BlockSpec((chans, cols), lambda y: (y, 0)),
                  pl.BlockSpec((chans, cols + DISP), lambda y: (y, 0))],
        out_specs=pl.BlockSpec((1, GROUPS, DISP, cols), lambda y: (y, 0, 0, 0)),
        name="correlate",
    )(tile, warped)
    return cost[None]


def solution(mesh):
    return jax.shard_map(
        shards,
        mesh=mesh,
        in_specs=(P("date", None, None, "col"), P("date", None, None), P("date", None), P("date")),
        out_specs=P("date", None, None, None, "col"),
        check_vma=False,
    )
```

```python
import functools

import jax
import jax.numpy as jnp
from jax import lax
from jax.experimental import pallas as pl
from jax.experimental.pallas import tpu as pltpu
from jax.sharding import PartitionSpec as P

GROUPS = 8
DISP = 128
SHIFTS = 3
EDGE = 16
PAD = 32
TAIL = 64
DMAX = 48
MESH = pl.DeviceIdType.MESH


def exchange_kernel(dates, col_count, rows, map_hbm, mask_hbm, disp_hbm, f_hbm, w_ref, fr_ref,
                    f_vm, map_ref, mask_ref, disp_ref, own, got, padf, part, left1, left2, right1, wt,
                    lsem, dsend, drecv, csend, crecv):
    date = lax.axis_index("date")
    col = lax.axis_index("col")
    yc, cols = f_hbm.shape
    chans = yc // rows
    reach = cols + 2 * EDGE

    def date_of(by):
        return lax.rem(date + by + dates, dates)

    def col_of(by):
        return lax.rem(col + by + col_count, col_count)

    barrier = pltpu.get_barrier_semaphore()
    for by in (-1, -2, -3):
        pl.semaphore_signal(barrier, inc=1, device_id={"date": date_of(by)}, device_id_type=MESH)
    for by in (-2, -1, 1):
        pl.semaphore_signal(barrier, inc=1, device_id={"col": col_of(by)}, device_id_type=MESH)
    loads = []
    for n, (src, dst) in enumerate(((f_hbm, f_vm), (map_hbm, map_ref), (mask_hbm, mask_ref), (disp_hbm, disp_ref))):
        copy = pltpu.make_async_copy(src, dst, lsem.at[n])
        copy.start()
        loads.append(copy)
    eye = (lax.broadcasted_iota(jnp.int32, (cols, cols), 0)
           == lax.broadcasted_iota(jnp.int32, (cols, cols), 1)).astype(jnp.bfloat16)
    for o in range(SHIFTS):
        padf[o, :PAD, :] = jnp.zeros((PAD, yc), jnp.float32)
        padf[o, PAD + cols:, :] = jnp.zeros((PAD, yc), jnp.float32)
    loads[0].wait()
    own[...] = lax.dot_general(eye, f_vm[...], (((1,), (1,)), ((), ())),
                               preferred_element_type=jnp.float32).astype(jnp.bfloat16)
    pl.semaphore_wait(barrier, 6)

    date_copies = [None] * SHIFTS
    for o in (2, 0, 1):
        copy = pltpu.make_async_remote_copy(
            src_ref=own, dst_ref=got.at[o], send_sem=dsend.at[o], recv_sem=drecv.at[o],
            device_id={"date": date_of(o + 1)}, device_id_type=MESH)
        copy.start()
        date_copies[o] = copy

    full = f_vm[...].astype(jnp.float32)
    fr_ref[0] = full
    for kb in range(1, DISP // 8):
        fr_ref[kb] = pltpu.roll(full, cols - 8 * kb, 1)
    for copy in loads[1:]:
        copy.wait()

    disp_first = disp_ref[0, 0]
    start = col * cols - EDGE - cols * col_count // 2
    row_ids = lax.broadcasted_iota(jnp.int32, (8, yc), 1) // chans
    sub_ids = lax.broadcasted_iota(jnp.int32, (8, yc), 0)
    for n, o in enumerate((1, 0, 2)):
        h0, h1, h2 = map_ref[o, 0, 0], map_ref[o, 0, 1], map_ref[o, 0, 2]
        base = h0 + h1 * start
        least = base + jnp.minimum(h1 * (reach - 1), 0) + jnp.minimum(h2 * (rows - 1), 0)
        shift = least >> 12
        first_row = PAD - EDGE + shift
        scale = mask_ref[0, o].astype(jnp.float32) * (GROUPS / chans)
        unit = scale / 4096.0
        numer = (base - shift * 4096) + h1 * sub_ids + h2 * row_ids
        ramp = numer.astype(jnp.float32) * unit
        step = (h1 * 8).astype(jnp.float32) * unit
        date_copies[o].wait_recv()
        padf[o, PAD:PAD + cols, :] = got[o].astype(jnp.float32)
        for i in range(reach // 8):
            e = ramp + step * float(i) if i else ramp
            w0 = jnp.maximum(scale - e, 0.0)
            w2 = jnp.maximum(e - scale, 0.0)
            w1 = scale - w0 - w2
            term = (w0 * padf[o, pl.ds(first_row + 8 * i, 8), :]
                    + w1 * padf[o, pl.ds(first_row + 8 * i + 1, 8), :]
                    + w2 * padf[o, pl.ds(first_row + 8 * i + 2, 8), :])
            if n == 0:
                part[pl.ds(8 * i, 8), :] = term
            else:
                part[pl.ds(8 * i, 8), :] += term

    col_copies = []
    for n, (src, size, dst, by) in enumerate((
            (0, reach, left1, 1),
            (reach - TAIL, TAIL, left2, 2),
            (0, EDGE, right1, -1))):
        copy = pltpu.make_async_remote_copy(
            src_ref=part.at[pl.ds(src, size)], dst_ref=dst, send_sem=csend.at[n], recv_sem=crecv.at[n],
            device_id={"col": col_of(by)}, device_id_type=MESH)
        copy.start()
        col_copies.append(copy)

    at1 = DMAX - EDGE
    at0 = at1 + cols
    at_r = at0 + cols
    wt[pl.ds(at0, cols + EDGE), :] = part[:cols + EDGE, :]
    for copy in col_copies:
        copy.wait_recv()
    over = TAIL - at1

    @pl.when(col > 1)
    def _():
        wt[:at1, :] = left2[:at1, :]
        wt[at1:at1 + over, :] = left2[at1:, :] + left1[:over, :]

    @pl.when(col == 1)
    def _():
        wt[:at1, :] = jnp.zeros((at1, yc), jnp.float32)
        wt[at1:at1 + over, :] = left1[:over, :]

    @pl.when(col > 0)
    def _():
        wt[at1 + over:at0, :] = left1[over:cols, :]
        wt[at0:at0 + 2 * EDGE, :] += left1[cols:, :]

    @pl.when(col == 0)
    def _():
        wt[:at0, :] = jnp.zeros((at0, yc), jnp.float32)

    @pl.when(col < col_count - 1)
    def _():
        wt[at_r:at_r + EDGE, :] += right1[...]

    for n in range((cols + DISP) // cols):
        w_ref[:, pl.ds(n * cols, cols)] = wt[pl.ds(DMAX - disp_first + n * cols, cols), :].T
    for copy in date_copies + col_copies:
        copy.wait_send()


def correlate_kernel(w_ref, fr_ref, o_hbm, buf, sem):
    total_groups, disps, cols = o_hbm.shape
    chans = w_ref.shape[0] // total_groups
    lanes = lax.broadcasted_iota(jnp.int32, (8, cols), 1)

    @pl.loop(0, total_groups, unroll=4)
    def _(g):
        lows, highs = [], []
        for c in range(chans):
            wide = jnp.broadcast_to(w_ref[pl.ds(g * chans + c, 1), :], (8, w_ref.shape[1]))
            skewed = pltpu.roll(wide, 0, 1, stride=1, stride_axis=0)
            lows.append(skewed[:, :cols])
            highs.append(skewed[:, cols:])
        blocks = []
        for kb in range(disps // 8):
            total = None
            for c in range(chans):
                tile = highs[c] if kb == 0 else jnp.where(lanes >= cols - 8 * kb, lows[c], highs[c])
                term = jnp.broadcast_to(fr_ref[kb, pl.ds(g * chans + c, 1), :], (8, cols)) * tile
                total = term if total is None else total + term
            blocks.append(pltpu.roll(total, 8 * kb, 1) if kb else total)
            if len(blocks) == 2:
                buf[g, pl.ds(8 * (kb - 1), 16), :] = jnp.concatenate(blocks, axis=0).astype(buf.dtype)
                blocks = []
        pltpu.make_async_copy(buf.at[g], o_hbm.at[g], sem).start()

    pltpu.make_async_copy(buf, o_hbm, sem).wait()


def shards(features, column_map, pair_mask, disp_start):
    rows, chans, cols = features.shape[1:]
    yc = rows * chans
    tile = features.reshape(yc, cols)
    dates, col_count = lax.axis_size("date"), lax.axis_size("col")
    anywhere = pl.BlockSpec(memory_space=pl.ANY)
    vmem = pl.BlockSpec(memory_space=pltpu.VMEM)
    reach = cols + 2 * EDGE
    warped, rolled = pl.pallas_call(
        functools.partial(exchange_kernel, dates, col_count, rows),
        out_shape=(pltpu.VMEM((yc, cols + DISP), jnp.float32),
                   pltpu.VMEM((DISP // 8, yc, cols), jnp.float32)),
        in_specs=[anywhere] * 4,
        out_specs=(vmem, vmem),
        scratch_shapes=[
            pltpu.VMEM((yc, cols), jnp.bfloat16),
            pltpu.SMEM((SHIFTS, 1, 3), jnp.int32),
            pltpu.SMEM((1, SHIFTS), jnp.int32),
            pltpu.SMEM((1, 1), jnp.int32),
            pltpu.VMEM((cols, yc), jnp.bfloat16),
            pltpu.VMEM((SHIFTS, cols, yc), jnp.bfloat16),
            pltpu.VMEM((SHIFTS, cols + 2 * PAD, yc), jnp.float32),
            pltpu.VMEM((reach, yc), jnp.float32),
            pltpu.VMEM((reach, yc), jnp.float32),
            pltpu.VMEM((TAIL, yc), jnp.float32),
            pltpu.VMEM((EDGE, yc), jnp.float32),
            pltpu.VMEM((DMAX + 2 * cols, yc), jnp.float32),
            pltpu.SemaphoreType.DMA((4,)),
            pltpu.SemaphoreType.DMA((SHIFTS,)),
            pltpu.SemaphoreType.DMA((SHIFTS,)),
            pltpu.SemaphoreType.DMA((3,)),
            pltpu.SemaphoreType.DMA((3,)),
        ],
        compiler_params=pltpu.CompilerParams(collective_id=0, has_side_effects=True),
        name="exchange",
    )(jnp.transpose(column_map, (1, 0, 2)), pair_mask, disp_start.reshape(1, 1), tile)
    warped = pltpu.with_memory_space_constraint(warped, pltpu.VMEM)
    rolled = pltpu.with_memory_space_constraint(rolled, pltpu.VMEM)
    cost = pl.pallas_call(
        correlate_kernel,
        out_shape=jax.ShapeDtypeStruct((rows * GROUPS, DISP, cols), jnp.bfloat16),
        in_specs=[vmem, vmem],
        out_specs=anywhere,
        scratch_shapes=[pltpu.VMEM((rows * GROUPS, DISP, cols), jnp.bfloat16), pltpu.SemaphoreType.DMA],
        name="correlate",
    )(warped, rolled)
    return cost.reshape(1, rows, GROUPS, DISP, cols)


def solution(mesh):
    return jax.shard_map(
        shards,
        mesh=mesh,
        in_specs=(P("date", None, None, "col"), P("date", None, None), P("date", None), P("date")),
        out_specs=P("date", None, None, None, "col"),
        check_vma=False,
    )
```

```python
import functools

import jax
import jax.numpy as jnp
from jax import lax
from jax.experimental import pallas as pl
from jax.experimental.pallas import tpu as pltpu
from jax.sharding import PartitionSpec as P

GROUPS = 8
DISP = 128
SHIFTS = 3
EDGE = 16
PAD = 32
TAIL = 48
DMAX = 32
MESH = pl.DeviceIdType.MESH


def exchange_kernel(dates, col_count, rows, map_hbm, mask_hbm, disp_hbm, f_hbm, w_ref, fr_ref,
                    f_vm, map_ref, mask_ref, disp_ref, got, padf, part, left1, left2, right1, wt,
                    lsem, dsend, drecv, csend, crecv):
    date = lax.axis_index("date")
    col = lax.axis_index("col")
    yc, cols = f_hbm.shape
    chans = yc // rows
    reach = cols + 2 * EDGE

    def date_of(by):
        return lax.rem(date + by + dates, dates)

    def col_of(by):
        return lax.rem(col + by + col_count, col_count)

    late = dates - SHIFTS
    barrier = pltpu.get_barrier_semaphore()
    for o in (1, 2, 3):
        @pl.when(date < late + o)
        def _():
            pl.semaphore_signal(barrier, inc=1, device_id={"date": date_of(-o)}, device_id_type=MESH)
    back = jnp.where(date > late, date - late + 1, 1)
    for by in (-2, -1, 1):
        @pl.when((col + by >= 0) & (col + by < col_count))
        def _():
            pl.semaphore_signal(barrier, inc=1, device_id={"date": date_of(-back), "col": col_of(by)},
                                device_id_type=MESH)
    loads = []
    for n, (src, dst) in enumerate(((f_hbm, f_vm), (map_hbm, map_ref), (mask_hbm, mask_ref), (disp_hbm, disp_ref))):
        copy = pltpu.make_async_copy(src, dst, lsem.at[n])
        copy.start()
        loads.append(copy)

    date_copies = []
    for o in range(SHIFTS):
        date_copies.append(pltpu.make_async_remote_copy(
            src_ref=f_hbm, dst_ref=got.at[o], send_sem=dsend.at[o], recv_sem=drecv.at[o],
            device_id={"date": date_of(o + 1)}, device_id_type=MESH))

    near = jnp.where(col > 0, 1, 0) + jnp.where(col < col_count - 1, 1, 0) + jnp.where(col < col_count - 2, 1, 0)
    for here, direct, beside in ((date < late - 1, 3, 1), (date == late - 1, 3, 3), (date == late, 1, 0),
                                 (date == late + 1, 2, 0), (date == late + 2, 3, 1)):
        @pl.when(here)
        def _():
            pl.semaphore_wait(barrier, direct + beside * near)
    for o in range(SHIFTS):
        @pl.when((date < late) | (date + o + 1 >= dates))
        def _():
            date_copies[o].start()

    eye = (lax.broadcasted_iota(jnp.int32, (cols, cols), 0)
           == lax.broadcasted_iota(jnp.int32, (cols, cols), 1)).astype(jnp.bfloat16)
    for o in range(SHIFTS):
        padf[o, :PAD, :] = jnp.zeros((PAD, yc), jnp.float32)
        padf[o, PAD + cols:, :] = jnp.zeros((PAD, yc), jnp.float32)
    loads[0].wait()
    full = f_vm[...].astype(jnp.float32)
    fr_ref[0] = full
    for kb in range(1, DISP // 8):
        fr_ref[kb] = pltpu.roll(full, cols - 8 * kb, 1)
    for copy in loads[1:]:
        copy.wait()

    disp_first = disp_ref[0, 0]
    start = col * cols - EDGE - cols * col_count // 2
    row_ids = lax.broadcasted_iota(jnp.int32, (8, yc), 1) // chans
    sub_ids = lax.broadcasted_iota(jnp.int32, (8, yc), 0)
    for n, o in enumerate((1, 0, 2)):
        h0, h1, h2 = map_ref[o, 0, 0], map_ref[o, 0, 1], map_ref[o, 0, 2]
        base = h0 + h1 * start
        least = base + jnp.minimum(h1 * (reach - 1), 0) + jnp.minimum(h2 * (rows - 1), 0)
        shift = least >> 12
        first_row = PAD - EDGE + shift
        scale = mask_ref[0, o].astype(jnp.float32) * (GROUPS / chans)
        unit = scale / 4096.0
        numer = (base - shift * 4096) + h1 * sub_ids + h2 * row_ids
        ramp = numer.astype(jnp.float32) * unit
        step = (h1 * 8).astype(jnp.float32) * unit
        date_copies[o].wait_recv()
        if o == 1:
            @pl.when((date == late) | (date == late + 1))
            def _():
                date_copies[0].start()
        if o == 0:
            @pl.when(date == late)
            def _():
                date_copies[1].start()
        padf[o, PAD:PAD + cols, :] = lax.dot_general(
            eye, got[o], (((1,), (1,)), ((), ())), preferred_element_type=jnp.float32)
        for i in range(reach // 8):
            e = ramp + step * float(i) if i else ramp
            w0 = jnp.maximum(scale - e, 0.0)
            w2 = jnp.maximum(e - scale, 0.0)
            w1 = scale - w0 - w2
            term = (w0 * padf[o, pl.ds(first_row + 8 * i, 8), :]
                    + w1 * padf[o, pl.ds(first_row + 8 * i + 1, 8), :]
                    + w2 * padf[o, pl.ds(first_row + 8 * i + 2, 8), :])
            if n == 0:
                part[pl.ds(8 * i, 8), :] = term
            else:
                part[pl.ds(8 * i, 8), :] += term

    col_copies = []
    for n, (src, size, dst, by) in enumerate((
            (0, reach, left1, 1),
            (reach - TAIL, TAIL, left2, 2),
            (0, EDGE, right1, -1))):
        copy = pltpu.make_async_remote_copy(
            src_ref=part.at[pl.ds(src, size)], dst_ref=dst, send_sem=csend.at[n], recv_sem=crecv.at[n],
            device_id={"col": col_of(by)}, device_id_type=MESH)
        sends = (col + by >= 0) & (col + by < col_count)
        comes = (col - by >= 0) & (col - by < col_count)
        pl.when(sends)(copy.start)
        col_copies.append((copy, sends, comes))

    at1 = DMAX - EDGE
    at0 = at1 + cols
    at_r = at0 + cols
    wt[pl.ds(at0, cols + EDGE), :] = part[:cols + EDGE, :]
    for copy, _, comes in col_copies:
        pl.when(comes)(copy.wait_recv)
    over = TAIL - at1

    @pl.when(col > 1)
    def _():
        wt[:at1, :] = left2[:at1, :]
        wt[at1:at1 + over, :] = left2[at1:, :] + left1[:over, :]

    @pl.when(col == 1)
    def _():
        wt[:at1, :] = jnp.zeros((at1, yc), jnp.float32)
        wt[at1:at1 + over, :] = left1[:over, :]

    @pl.when(col > 0)
    def _():
        wt[at1 + over:at0, :] = left1[over:cols, :]
        wt[at0:at0 + 2 * EDGE, :] += left1[cols:, :]

    @pl.when(col == 0)
    def _():
        wt[:at0, :] = jnp.zeros((at0, yc), jnp.float32)

    @pl.when(col < col_count - 1)
    def _():
        wt[at_r:at_r + EDGE, :] += right1[...]

    for n in range((cols + DISP) // cols):
        w_ref[:, pl.ds(n * cols, cols)] = wt[pl.ds(DMAX - disp_first + n * cols, cols), :].T
    for copy in date_copies:
        copy.wait_send()
    for copy, sends, _ in col_copies:
        pl.when(sends)(copy.wait_send)


def correlate_kernel(w_ref, fr_ref, o_hbm, buf, sem):
    total_groups, disps, cols = o_hbm.shape
    chans = w_ref.shape[0] // total_groups
    lanes = lax.broadcasted_iota(jnp.int32, (8, cols), 1)

    @pl.loop(0, total_groups, unroll=4)
    def _(g):
        lows, highs = [], []
        for c in range(chans):
            wide = jnp.broadcast_to(w_ref[pl.ds(g * chans + c, 1), :], (8, w_ref.shape[1]))
            skewed = pltpu.roll(wide, 0, 1, stride=1, stride_axis=0)
            lows.append(skewed[:, :cols])
            highs.append(skewed[:, cols:])
        blocks = []
        for kb in range(disps // 8):
            total = None
            for c in range(chans):
                tile = highs[c] if kb == 0 else jnp.where(lanes >= cols - 8 * kb, lows[c], highs[c])
                term = jnp.broadcast_to(fr_ref[kb, pl.ds(g * chans + c, 1), :], (8, cols)) * tile
                total = term if total is None else total + term
            blocks.append(pltpu.roll(total, 8 * kb, 1) if kb else total)
            if len(blocks) == 2:
                buf[g, pl.ds(8 * (kb - 1), 16), :] = jnp.concatenate(blocks, axis=0).astype(buf.dtype)
                blocks = []
        pltpu.make_async_copy(buf.at[g], o_hbm.at[g], sem).start()

    pltpu.make_async_copy(buf, o_hbm, sem).wait()


def shards(features, column_map, pair_mask, disp_start):
    rows, chans, cols = features.shape[1:]
    yc = rows * chans
    tile = features.reshape(yc, cols)
    dates, col_count = lax.axis_size("date"), lax.axis_size("col")
    anywhere = pl.BlockSpec(memory_space=pl.ANY)
    vmem = pl.BlockSpec(memory_space=pltpu.VMEM)
    reach = cols + 2 * EDGE
    warped, rolled = pl.pallas_call(
        functools.partial(exchange_kernel, dates, col_count, rows),
        out_shape=(pltpu.VMEM((yc, cols + DISP), jnp.float32),
                   pltpu.VMEM((DISP // 8, yc, cols), jnp.float32)),
        in_specs=[anywhere] * 4,
        out_specs=(vmem, vmem),
        scratch_shapes=[
            pltpu.VMEM((yc, cols), jnp.bfloat16),
            pltpu.SMEM((SHIFTS, 1, 3), jnp.int32),
            pltpu.SMEM((1, SHIFTS), jnp.int32),
            pltpu.SMEM((1, 1), jnp.int32),
            pltpu.VMEM((SHIFTS, yc, cols), jnp.bfloat16),
            pltpu.VMEM((SHIFTS, cols + 2 * PAD, yc), jnp.float32),
            pltpu.VMEM((reach, yc), jnp.float32),
            pltpu.VMEM((reach, yc), jnp.float32),
            pltpu.VMEM((TAIL, yc), jnp.float32),
            pltpu.VMEM((EDGE, yc), jnp.float32),
            pltpu.VMEM((DMAX + 2 * cols, yc), jnp.float32),
            pltpu.SemaphoreType.DMA((4,)),
            pltpu.SemaphoreType.DMA((SHIFTS,)),
            pltpu.SemaphoreType.DMA((SHIFTS,)),
            pltpu.SemaphoreType.DMA((3,)),
            pltpu.SemaphoreType.DMA((3,)),
        ],
        compiler_params=pltpu.CompilerParams(collective_id=0, has_side_effects=True),
        name="exchange",
    )(jnp.transpose(column_map, (1, 0, 2)), pair_mask, disp_start.reshape(1, 1), tile)
    warped = pltpu.with_memory_space_constraint(warped, pltpu.VMEM)
    rolled = pltpu.with_memory_space_constraint(rolled, pltpu.VMEM)
    cost = pl.pallas_call(
        correlate_kernel,
        out_shape=jax.ShapeDtypeStruct((rows * GROUPS, DISP, cols), jnp.bfloat16),
        in_specs=[vmem, vmem],
        out_specs=anywhere,
        scratch_shapes=[pltpu.VMEM((rows * GROUPS, DISP, cols), jnp.bfloat16), pltpu.SemaphoreType.DMA],
        name="correlate",
    )(warped, rolled)
    return cost.reshape(1, rows, GROUPS, DISP, cols)


def solution(mesh):
    return jax.shard_map(
        shards,
        mesh=mesh,
        in_specs=(P("date", None, None, "col"), P("date", None, None), P("date", None), P("date")),
        out_specs=P("date", None, None, None, "col"),
        check_vma=False,
    )
```

```python
import functools

import jax
import jax.numpy as jnp
from jax import lax
from jax.experimental import pallas as pl
from jax.experimental.pallas import tpu as pltpu
from jax.sharding import PartitionSpec as P

GROUPS = 8
DISP = 128
SHIFTS = 3
EDGE = 16
PAD = 32
TAIL = 48
DMAX = 32
BATCH = 4
MESH = pl.DeviceIdType.MESH


def exchange_kernel(dates, col_count, rows, map_hbm, mask_hbm, disp_hbm, f_hbm, w_ref, fr_ref,
                    f_vm, map_ref, mask_ref, disp_ref, got, padf, part, left1, left2, right1, wt,
                    lsem, dsend, drecv, csend, crecv, ready):
    date = lax.axis_index("date")
    col = lax.axis_index("col")
    yc, cols = f_hbm.shape
    chans = yc // rows
    reach = cols + 2 * EDGE

    def date_before(by):
        return jnp.where(date < by, date - by + dates, date - by)

    def date_after(by):
        return jnp.where(date + by >= dates, date + by - dates, date + by)

    def col_of(by):
        return jnp.clip(col + by, 0, col_count - 1)

    late = dates - SHIFTS
    last = dates - 1
    barrier = pltpu.get_barrier_semaphore()
    for o in (1, 2, 3):
        @pl.when(date < late + o)
        def _():
            pl.semaphore_signal(barrier, inc=1, device_id={"date": date_before(o)}, device_id_type=MESH)

    @pl.when(date == last)
    def _():
        pl.semaphore_signal(barrier, inc=1, device_id={"date": date_before(4)}, device_id_type=MESH)

    back = jnp.where(date >= late, date - late + 1, 2)
    for by in (-2, -1, 1):
        @pl.when((col + by >= 0) & (col + by < col_count))
        def _():
            pl.semaphore_signal(barrier, inc=1, device_id={"date": date_before(back), "col": col_of(by)},
                                device_id_type=MESH)

    near = jnp.where(col > 0, 1, 0) + jnp.where(col < col_count - 1, 1, 0) + jnp.where(col < col_count - 2, 1, 0)
    for here, direct, beside in ((date < last - 4, 3, 1), (date == last - 4, 4, 0), (date == last - 3, 3, 3),
                                 (date == last - 2, 1, 0), (date == last - 1, 2, 1), (date == last, 3, 1)):
        @pl.when(here)
        def _():
            pl.semaphore_wait(barrier, direct + beside * near)
    date_copies = []
    for o in range(SHIFTS):
        date_copies.append(pltpu.make_async_remote_copy(
            src_ref=f_hbm, dst_ref=got.at[o], send_sem=dsend.at[o], recv_sem=drecv.at[o],
            device_id={"date": date_after(o + 1)}, device_id_type=MESH))
    for o in (2, 0, 1):
        date_copies[o].start() if o == 2 else pl.when((date < late) | (date + o + 1 >= dates))(date_copies[o].start)

    @pl.when(date == last - 4)
    def _():
        for by in (2, 3):
            pl.semaphore_signal(ready, inc=1, device_id={"date": date_after(by)}, device_id_type=MESH)

    loads = []
    for n, (src, dst) in enumerate(((f_hbm, f_vm), (map_hbm, map_ref), (mask_hbm, mask_ref), (disp_hbm, disp_ref))):
        copy = pltpu.make_async_copy(src, dst, lsem.at[n])
        copy.start()
        loads.append(copy)

    @pl.when((date == late) | (date == late + 1))
    def _():
        pl.semaphore_wait(ready, 1)
        date_copies[0].start()

    pl.when(date == late)(date_copies[1].start)

    eye = (lax.broadcasted_iota(jnp.int32, (cols, cols), 0)
           == lax.broadcasted_iota(jnp.int32, (cols, cols), 1)).astype(jnp.bfloat16)
    for o in range(SHIFTS):
        padf[o, :PAD, :] = jnp.zeros((PAD, yc), jnp.float32)
        padf[o, PAD + cols:, :] = jnp.zeros((PAD, yc), jnp.float32)
    loads[0].wait()
    full = f_vm[...].astype(jnp.float32)
    fr_ref[0] = full
    for kb in range(1, DISP // 8):
        fr_ref[kb] = pltpu.roll(full, cols - 8 * kb, 1)
    for copy in loads[1:]:
        copy.wait()

    disp_first = disp_ref[0, 0]
    start = col * cols - EDGE - cols * col_count // 2
    row_ids = lax.broadcasted_iota(jnp.int32, (8, yc), 1) // chans
    sub_ids = lax.broadcasted_iota(jnp.int32, (8, yc), 0)
    for n, o in enumerate((1, 0, 2)):
        h0, h1, h2 = map_ref[o, 0, 0], map_ref[o, 0, 1], map_ref[o, 0, 2]
        base = h0 + h1 * start
        least = base + jnp.minimum(h1 * (reach - 1), 0) + jnp.minimum(h2 * (rows - 1), 0)
        shift = least >> 12
        first_row = PAD - EDGE + shift
        scale = mask_ref[0, o].astype(jnp.float32) * (GROUPS / chans)
        unit = scale / 4096.0
        numer = (base - shift * 4096) + h1 * sub_ids + h2 * row_ids
        ramp = numer.astype(jnp.float32) * unit
        step = (h1 * 8).astype(jnp.float32) * unit
        date_copies[o].wait_recv()
        padf[o, PAD:PAD + cols, :] = lax.dot_general(
            eye, got[o], (((1,), (1,)), ((), ())), preferred_element_type=jnp.float32)
        for i in range(reach // 8):
            e = ramp + step * float(i) if i else ramp
            w0 = jnp.maximum(scale - e, 0.0)
            w2 = jnp.maximum(e - scale, 0.0)
            w1 = scale - w0 - w2
            term = (w0 * padf[o, pl.ds(first_row + 8 * i, 8), :]
                    + w1 * padf[o, pl.ds(first_row + 8 * i + 1, 8), :]
                    + w2 * padf[o, pl.ds(first_row + 8 * i + 2, 8), :])
            if n == 0:
                part[pl.ds(8 * i, 8), :] = term
            else:
                part[pl.ds(8 * i, 8), :] += term

    col_copies = []
    for n, (src, size, dst, by) in enumerate((
            (0, reach, left1, 1),
            (reach - TAIL, TAIL, left2, 2),
            (0, EDGE, right1, -1))):
        copy = pltpu.make_async_remote_copy(
            src_ref=part.at[pl.ds(src, size)], dst_ref=dst, send_sem=csend.at[n], recv_sem=crecv.at[n],
            device_id={"col": col_of(by)}, device_id_type=MESH)
        sends = (col + by >= 0) & (col + by < col_count)
        comes = (col - by >= 0) & (col - by < col_count)
        pl.when(sends)(copy.start)
        col_copies.append((copy, sends, comes))

    at1 = DMAX - EDGE
    at0 = at1 + cols
    at_r = at0 + cols
    wt[pl.ds(at0, cols + EDGE), :] = part[:cols + EDGE, :]
    for copy, _, comes in col_copies:
        pl.when(comes)(copy.wait_recv)
    over = TAIL - at1

    @pl.when(col > 1)
    def _():
        wt[:at1, :] = left2[:at1, :]
        wt[at1:at1 + over, :] = left2[at1:, :] + left1[:over, :]

    @pl.when(col == 1)
    def _():
        wt[:at1, :] = jnp.zeros((at1, yc), jnp.float32)
        wt[at1:at1 + over, :] = left1[:over, :]

    @pl.when(col > 0)
    def _():
        wt[at1 + over:at0, :] = left1[over:cols, :]
        wt[at0:at0 + 2 * EDGE, :] += left1[cols:, :]

    @pl.when(col == 0)
    def _():
        wt[:at0, :] = jnp.zeros((at0, yc), jnp.float32)

    @pl.when(col < col_count - 1)
    def _():
        wt[at_r:at_r + EDGE, :] += right1[...]

    for n in range((cols + DISP) // cols):
        w_ref[:, pl.ds(n * cols, cols)] = wt[pl.ds(DMAX - disp_first + n * cols, cols), :].T
    for copy in date_copies:
        copy.wait_send()
    for copy, sends, _ in col_copies:
        pl.when(sends)(copy.wait_send)


def correlate_kernel(w_ref, fr_ref, o_hbm, buf, even, odd, sem):
    total_groups, disps, cols = o_hbm.shape
    chans = w_ref.shape[0] // total_groups
    batch = even.shape[0] // chans
    batches = total_groups // batch
    lanes = lax.broadcasted_iota(jnp.int32, (8, cols), 1)

    def skew(into, which):
        for n in range(batch * chans):
            wide = jnp.broadcast_to(w_ref[pl.ds(which * batch * chans + n, 1), :], (8, w_ref.shape[1]))
            skewed = pltpu.roll(wide, 0, 1, stride=1, stride_axis=0)
            into[n, 0] = skewed[:, :cols]
            into[n, 1] = skewed[:, cols:]

    def score(held, which):
        for q in range(batch):
            g = which * batch + q
            lows = [held[q * chans + c, 0] for c in range(chans)]
            highs = [held[q * chans + c, 1] for c in range(chans)]
            blocks = []
            for kb in range(disps // 8):
                total = None
                for c in range(chans):
                    tile = highs[c] if kb == 0 else jnp.where(lanes >= cols - 8 * kb, lows[c], highs[c])
                    term = jnp.broadcast_to(fr_ref[kb, pl.ds(g * chans + c, 1), :], (8, cols)) * tile
                    total = term if total is None else total + term
                blocks.append(pltpu.roll(total, 8 * kb, 1) if kb else total)
                if len(blocks) == 2:
                    buf[g, pl.ds(8 * (kb - 1), 16), :] = jnp.concatenate(blocks, axis=0).astype(buf.dtype)
                    blocks = []
        here = pl.ds(which * batch, batch)
        pltpu.make_async_copy(buf.at[here], o_hbm.at[here], sem).start()

    skew(even, 0)

    @pl.loop(0, batches // 2)
    def _(n):
        skew(odd, 2 * n + 1)
        score(even, 2 * n)
        skew(even, jnp.minimum(2 * n + 2, batches - 1))
        score(odd, 2 * n + 1)

    pltpu.make_async_copy(buf, o_hbm, sem).wait()


def shards(features, column_map, pair_mask, disp_start):
    rows, chans, cols = features.shape[1:]
    yc = rows * chans
    tile = features.reshape(yc, cols)
    dates, col_count = lax.axis_size("date"), lax.axis_size("col")
    anywhere = pl.BlockSpec(memory_space=pl.ANY)
    vmem = pl.BlockSpec(memory_space=pltpu.VMEM)
    reach = cols + 2 * EDGE
    warped, rolled = pl.pallas_call(
        functools.partial(exchange_kernel, dates, col_count, rows),
        out_shape=(pltpu.VMEM((yc, cols + DISP), jnp.float32),
                   pltpu.VMEM((DISP // 8, yc, cols), jnp.float32)),
        in_specs=[anywhere] * 4,
        out_specs=(vmem, vmem),
        scratch_shapes=[
            pltpu.VMEM((yc, cols), jnp.bfloat16),
            pltpu.SMEM((SHIFTS, 1, 3), jnp.int32),
            pltpu.SMEM((1, SHIFTS), jnp.int32),
            pltpu.SMEM((1, 1), jnp.int32),
            pltpu.VMEM((SHIFTS, yc, cols), jnp.bfloat16),
            pltpu.VMEM((SHIFTS, cols + 2 * PAD, yc), jnp.float32),
            pltpu.VMEM((reach, yc), jnp.float32),
            pltpu.VMEM((reach, yc), jnp.float32),
            pltpu.VMEM((TAIL, yc), jnp.float32),
            pltpu.VMEM((EDGE, yc), jnp.float32),
            pltpu.VMEM((DMAX + 2 * cols, yc), jnp.float32),
            pltpu.SemaphoreType.DMA((4,)),
            pltpu.SemaphoreType.DMA((SHIFTS,)),
            pltpu.SemaphoreType.DMA((SHIFTS,)),
            pltpu.SemaphoreType.DMA((3,)),
            pltpu.SemaphoreType.DMA((3,)),
            pltpu.SemaphoreType.REGULAR,
        ],
        compiler_params=pltpu.CompilerParams(collective_id=0, has_side_effects=True),
        name="exchange",
    )(jnp.transpose(column_map, (1, 0, 2)), pair_mask, disp_start.reshape(1, 1), tile)
    warped = pltpu.with_memory_space_constraint(warped, pltpu.VMEM)
    rolled = pltpu.with_memory_space_constraint(rolled, pltpu.VMEM)
    cost = pl.pallas_call(
        correlate_kernel,
        out_shape=jax.ShapeDtypeStruct((rows * GROUPS, DISP, cols), jnp.bfloat16),
        in_specs=[vmem, vmem],
        out_specs=anywhere,
        scratch_shapes=[
            pltpu.VMEM((rows * GROUPS, DISP, cols), jnp.bfloat16),
            pltpu.VMEM((BATCH * chans // GROUPS, 2, 8, cols), jnp.float32),
            pltpu.VMEM((BATCH * chans // GROUPS, 2, 8, cols), jnp.float32),
            pltpu.SemaphoreType.DMA,
        ],
        name="correlate",
    )(warped, rolled)
    return cost.reshape(1, rows, GROUPS, DISP, cols)


def solution(mesh):
    return jax.shard_map(
        shards,
        mesh=mesh,
        in_specs=(P("date", None, None, "col"), P("date", None, None), P("date", None), P("date")),
        out_specs=P("date", None, None, None, "col"),
        check_vma=False,
    )
```

```python
import functools

import jax
import jax.numpy as jnp
from jax import lax
from jax.experimental import pallas as pl
from jax.experimental.pallas import tpu as pltpu
from jax.sharding import PartitionSpec as P

GROUPS = 8
DISP = 128
SHIFTS = 3
EDGE = 16
PAD = 32
TAIL = 48
DMAX = 32
BATCH = 4
MESH = pl.DeviceIdType.MESH


def exchange_kernel(dates, col_count, rows, map_hbm, mask_hbm, f_hbm, wt, fr_ref,
                    f_vm, map_ref, mask_ref, got, padf, part, left1, left2, right1,
                    lsem, dsend, drecv, csend, crecv, ready):
    date = lax.axis_index("date")
    col = lax.axis_index("col")
    yc, cols = f_hbm.shape
    chans = yc // rows
    reach = cols + 2 * EDGE

    def date_before(by):
        return jnp.where(date < by, date - by + dates, date - by)

    def date_after(by):
        return jnp.where(date + by >= dates, date + by - dates, date + by)

    def col_of(by):
        return jnp.clip(col + by, 0, col_count - 1)

    late = dates - SHIFTS
    last = dates - 1
    barrier = pltpu.get_barrier_semaphore()
    for o in (1, 2, 3):
        @pl.when(date < late + o)
        def _():
            pl.semaphore_signal(barrier, inc=1, device_id={"date": date_before(o)}, device_id_type=MESH)

    @pl.when(date == last)
    def _():
        pl.semaphore_signal(barrier, inc=1, device_id={"date": date_before(4)}, device_id_type=MESH)

    back = jnp.where(date >= late, date - late + 1, 2)
    for by in (-2, -1, 1):
        @pl.when((col + by >= 0) & (col + by < col_count))
        def _():
            pl.semaphore_signal(barrier, inc=1, device_id={"date": date_before(back), "col": col_of(by)},
                                device_id_type=MESH)

    near = jnp.where(col > 0, 1, 0) + jnp.where(col < col_count - 1, 1, 0) + jnp.where(col < col_count - 2, 1, 0)
    for here, direct, beside in ((date < last - 4, 3, 1), (date == last - 4, 4, 0), (date == last - 3, 3, 3),
                                 (date == last - 2, 1, 0), (date == last - 1, 2, 1), (date == last, 3, 1)):
        @pl.when(here)
        def _():
            pl.semaphore_wait(barrier, direct + beside * near)
    date_copies = []
    for o in range(SHIFTS):
        date_copies.append(pltpu.make_async_remote_copy(
            src_ref=f_hbm, dst_ref=got.at[o], send_sem=dsend.at[o], recv_sem=drecv.at[o],
            device_id={"date": date_after(o + 1)}, device_id_type=MESH))
    for o in (2, 0, 1):
        date_copies[o].start() if o == 2 else pl.when((date < late) | (date + o + 1 >= dates))(date_copies[o].start)

    @pl.when(date == last - 4)
    def _():
        for by in (2, 3):
            pl.semaphore_signal(ready, inc=1, device_id={"date": date_after(by)}, device_id_type=MESH)

    loads = []
    for n, (src, dst) in enumerate(((f_hbm, f_vm), (map_hbm, map_ref), (mask_hbm, mask_ref))):
        copy = pltpu.make_async_copy(src, dst, lsem.at[n])
        copy.start()
        loads.append(copy)

    @pl.when((date == late) | (date == late + 1))
    def _():
        pl.semaphore_wait(ready, 1)
        date_copies[0].start()

    pl.when(date == late)(date_copies[1].start)

    eye = (lax.broadcasted_iota(jnp.int32, (cols, cols), 0)
           == lax.broadcasted_iota(jnp.int32, (cols, cols), 1)).astype(jnp.bfloat16)
    for o in range(SHIFTS):
        padf[o, :PAD, :] = jnp.zeros((PAD, yc), jnp.float32)
        padf[o, PAD + cols:, :] = jnp.zeros((PAD, yc), jnp.float32)
    loads[0].wait()
    full = f_vm[...].astype(jnp.float32)
    fr_ref[0] = full
    for kb in range(1, DISP // 8):
        fr_ref[kb] = pltpu.roll(full, cols - 8 * kb, 1)
    for copy in loads[1:]:
        copy.wait()

    start = col * cols - EDGE - cols * col_count // 2
    row_ids = lax.broadcasted_iota(jnp.int32, (8, yc), 1) // chans
    sub_ids = lax.broadcasted_iota(jnp.int32, (8, yc), 0)
    for n, o in enumerate((1, 0, 2)):
        h0, h1, h2 = map_ref[o, 0, 0], map_ref[o, 0, 1], map_ref[o, 0, 2]
        base = h0 + h1 * start
        least = base + jnp.minimum(h1 * (reach - 1), 0) + jnp.minimum(h2 * (rows - 1), 0)
        shift = least >> 12
        first_row = PAD - EDGE + shift
        scale = mask_ref[0, o].astype(jnp.float32) * (GROUPS / chans)
        unit = scale / 4096.0
        numer = (base - shift * 4096) + h1 * sub_ids + h2 * row_ids
        ramp = numer.astype(jnp.float32) * unit
        step = (h1 * 8).astype(jnp.float32) * unit
        date_copies[o].wait_recv()
        padf[o, PAD:PAD + cols, :] = lax.dot_general(
            eye, got[o], (((1,), (1,)), ((), ())), preferred_element_type=jnp.float32)
        for i in range(reach // 8):
            e = ramp + step * float(i) if i else ramp
            w0 = jnp.maximum(scale - e, 0.0)
            w2 = jnp.maximum(e - scale, 0.0)
            w1 = scale - w0 - w2
            term = (w0 * padf[o, pl.ds(first_row + 8 * i, 8), :]
                    + w1 * padf[o, pl.ds(first_row + 8 * i + 1, 8), :]
                    + w2 * padf[o, pl.ds(first_row + 8 * i + 2, 8), :])
            if n == 0:
                part[pl.ds(8 * i, 8), :] = term
            else:
                part[pl.ds(8 * i, 8), :] += term

    col_copies = []
    for n, (src, size, dst, by) in enumerate((
            (0, reach, left1, 1),
            (reach - TAIL, TAIL, left2, 2),
            (0, EDGE, right1, -1))):
        copy = pltpu.make_async_remote_copy(
            src_ref=part.at[pl.ds(src, size)], dst_ref=dst, send_sem=csend.at[n], recv_sem=crecv.at[n],
            device_id={"col": col_of(by)}, device_id_type=MESH)
        sends = (col + by >= 0) & (col + by < col_count)
        comes = (col - by >= 0) & (col - by < col_count)
        pl.when(sends)(copy.start)
        col_copies.append((copy, sends, comes))

    at1 = DMAX - EDGE
    at0 = at1 + cols
    at_r = at0 + cols
    wt[pl.ds(at0, cols + EDGE), :] = part[:cols + EDGE, :]
    for copy, _, comes in col_copies:
        pl.when(comes)(copy.wait_recv)
    over = TAIL - at1

    @pl.when(col > 1)
    def _():
        wt[:at1, :] = left2[:at1, :]
        wt[at1:at1 + over, :] = left2[at1:, :] + left1[:over, :]

    @pl.when(col == 1)
    def _():
        wt[:at1, :] = jnp.zeros((at1, yc), jnp.float32)
        wt[at1:at1 + over, :] = left1[:over, :]

    @pl.when(col > 0)
    def _():
        wt[at1 + over:at0, :] = left1[over:cols, :]
        wt[at0:at0 + 2 * EDGE, :] += left1[cols:, :]

    @pl.when(col == 0)
    def _():
        wt[:at0, :] = jnp.zeros((at0, yc), jnp.float32)

    @pl.when(col < col_count - 1)
    def _():
        wt[at_r:at_r + EDGE, :] += right1[...]

    for copy in date_copies:
        copy.wait_send()
    for copy, sends, _ in col_copies:
        pl.when(sends)(copy.wait_send)


def correlate_kernel(disp_ref, wt_ref, fr_ref, o_hbm, w_ref, buf, even, odd, sem):
    total_groups, disps, cols = o_hbm.shape
    chans = w_ref.shape[0] // total_groups
    batch = even.shape[0] // chans
    batches = total_groups // batch
    lanes = lax.broadcasted_iota(jnp.int32, (8, cols), 1)

    def skew(into, which):
        for n in range(batch * chans):
            wide = jnp.broadcast_to(w_ref[pl.ds(which * batch * chans + n, 1), :], (8, w_ref.shape[1]))
            skewed = pltpu.roll(wide, 0, 1, stride=1, stride_axis=0)
            into[n, 0] = skewed[:, :cols]
            into[n, 1] = skewed[:, cols:]

    def score(held, which):
        for q in range(batch):
            g = which * batch + q
            lows = [held[q * chans + c, 0] for c in range(chans)]
            highs = [held[q * chans + c, 1] for c in range(chans)]
            blocks = []
            for kb in range(disps // 8):
                total = None
                for c in range(chans):
                    tile = highs[c] if kb == 0 else jnp.where(lanes >= cols - 8 * kb, lows[c], highs[c])
                    term = jnp.broadcast_to(fr_ref[kb, pl.ds(g * chans + c, 1), :], (8, cols)) * tile
                    total = term if total is None else total + term
                blocks.append(pltpu.roll(total, 8 * kb, 1) if kb else total)
                if len(blocks) == 2:
                    buf[g, pl.ds(8 * (kb - 1), 16), :] = jnp.concatenate(blocks, axis=0).astype(buf.dtype)
                    blocks = []
            pltpu.make_async_copy(buf.at[g], o_hbm.at[g], sem).start()

    for n in range((cols + DISP) // cols):
        w_ref[:, pl.ds(n * cols, cols)] = wt_ref[pl.ds(DMAX - disp_ref[0] + n * cols, cols), :].T
    skew(even, 0)

    for n in range(batches // 2):
        skew(odd, 2 * n + 1)
        score(even, 2 * n)
        if n + 1 < batches // 2:
            skew(even, 2 * n + 2)
        score(odd, 2 * n + 1)

    pltpu.make_async_copy(buf, o_hbm, sem).wait()


def shards(features, column_map, pair_mask, disp_start):
    rows, chans, cols = features.shape[1:]
    yc = rows * chans
    tile = features.reshape(yc, cols)
    dates, col_count = lax.axis_size("date"), lax.axis_size("col")
    anywhere = pl.BlockSpec(memory_space=pl.ANY)
    vmem = pl.BlockSpec(memory_space=pltpu.VMEM)
    reach = cols + 2 * EDGE
    warped, rolled = pl.pallas_call(
        functools.partial(exchange_kernel, dates, col_count, rows),
        out_shape=(pltpu.VMEM((DMAX + 2 * cols, yc), jnp.float32),
                   pltpu.VMEM((DISP // 8, yc, cols), jnp.float32)),
        in_specs=[anywhere] * 3,
        out_specs=(vmem, vmem),
        scratch_shapes=[
            pltpu.VMEM((yc, cols), jnp.bfloat16),
            pltpu.SMEM((SHIFTS, 1, 3), jnp.int32),
            pltpu.SMEM((1, SHIFTS), jnp.int32),
            pltpu.VMEM((SHIFTS, yc, cols), jnp.bfloat16),
            pltpu.VMEM((SHIFTS, cols + 2 * PAD, yc), jnp.float32),
            pltpu.VMEM((reach, yc), jnp.float32),
            pltpu.VMEM((reach, yc), jnp.float32),
            pltpu.VMEM((TAIL, yc), jnp.float32),
            pltpu.VMEM((EDGE, yc), jnp.float32),
            pltpu.SemaphoreType.DMA((3,)),
            pltpu.SemaphoreType.DMA((SHIFTS,)),
            pltpu.SemaphoreType.DMA((SHIFTS,)),
            pltpu.SemaphoreType.DMA((3,)),
            pltpu.SemaphoreType.DMA((3,)),
            pltpu.SemaphoreType.REGULAR,
        ],
        compiler_params=pltpu.CompilerParams(collective_id=0, has_side_effects=True),
        name="exchange",
    )(jnp.transpose(column_map, (1, 0, 2)), pair_mask, tile)
    warped = pltpu.with_memory_space_constraint(warped, pltpu.VMEM)
    rolled = pltpu.with_memory_space_constraint(rolled, pltpu.VMEM)
    cost = pl.pallas_call(
        correlate_kernel,
        out_shape=jax.ShapeDtypeStruct((rows * GROUPS, DISP, cols), jnp.bfloat16),
        in_specs=[pl.BlockSpec(memory_space=pltpu.SMEM), vmem, vmem],
        out_specs=anywhere,
        scratch_shapes=[
            pltpu.VMEM((yc, cols + DISP), jnp.float32),
            pltpu.VMEM((rows * GROUPS, DISP, cols), jnp.bfloat16),
            pltpu.VMEM((BATCH * chans // GROUPS, 2, 8, cols), jnp.float32),
            pltpu.VMEM((BATCH * chans // GROUPS, 2, 8, cols), jnp.float32),
            pltpu.SemaphoreType.DMA,
        ],
        name="correlate",
    )(disp_start, warped, rolled)
    return cost.reshape(1, rows, GROUPS, DISP, cols)


def solution(mesh):
    return jax.shard_map(
        shards,
        mesh=mesh,
        in_specs=(P("date", None, None, "col"), P("date", None, None), P("date", None), P("date")),
        out_specs=P("date", None, None, None, "col"),
        check_vma=False,
    )
```

```python
import functools

import jax
import jax.numpy as jnp
from jax import lax
from jax.experimental import pallas as pl
from jax.experimental.pallas import tpu as pltpu
from jax.sharding import PartitionSpec as P

GROUPS = 8
DISP = 128
SHIFTS = 3
EDGE = 16
PAD = 32
TAIL = 48
DMAX = 32
BATCH = 4
MESH = pl.DeviceIdType.MESH


def exchange_kernel(dates, col_count, rows, map_hbm, mask_hbm, f_hbm, wt, fr_ref,
                    f_vm, map_ref, mask_ref, got, padf, part, left1, left2, right1,
                    lsem, dsend, drecv, csend, crecv, ready):
    date = lax.axis_index("date")
    col = lax.axis_index("col")
    yc, cols = f_hbm.shape
    chans = yc // rows
    reach = cols + 2 * EDGE

    def date_before(by):
        return jnp.where(date < by, date - by + dates, date - by)

    def date_after(by):
        return jnp.where(date + by >= dates, date + by - dates, date + by)

    def col_of(by):
        return jnp.clip(col + by, 0, col_count - 1)

    late = dates - SHIFTS
    last = dates - 1
    barrier = pltpu.get_barrier_semaphore()
    near = jnp.where(col > 0, 1, 0) + jnp.where(col < col_count - 1, 1, 0) + jnp.where(col < col_count - 2, 1, 0)
    date_copies = []
    for o in range(SHIFTS):
        date_copies.append(pltpu.make_async_remote_copy(
            src_ref=f_hbm, dst_ref=got.at[o], send_sem=dsend.at[o], recv_sem=drecv.at[o],
            device_id={"date": date_after(o + 1)}, device_id_type=MESH))

    @pl.when(date >= late)
    def _():
        for here, direct, beside in ((date == late, 1, 0), (date == late + 1, 2, 1), (date == last, 3, 1)):
            @pl.when(here)
            def _():
                pl.semaphore_wait(barrier, direct + beside * near)
        for o in (2, 0, 1):
            pl.when(date + o + 1 >= dates)(date_copies[o].start)

    for o in (1, 2, 3):
        @pl.when(date < late + o)
        def _():
            pl.semaphore_signal(barrier, inc=1, device_id={"date": date_before(o)}, device_id_type=MESH)

    @pl.when(date == last)
    def _():
        pl.semaphore_signal(barrier, inc=1, device_id={"date": date_before(4)}, device_id_type=MESH)

    back = jnp.where(date >= late, date - late + 1, 2)
    for by in (-2, -1, 1):
        @pl.when((col + by >= 0) & (col + by < col_count))
        def _():
            pl.semaphore_signal(barrier, inc=1, device_id={"date": date_before(back), "col": col_of(by)},
                                device_id_type=MESH)

    @pl.when(date < late)
    def _():
        for here, direct, beside in ((date < last - 4, 3, 1), (date == last - 4, 4, 0), (date == last - 3, 3, 3)):
            @pl.when(here)
            def _():
                pl.semaphore_wait(barrier, direct + beside * near)
        for o in (2, 0, 1):
            date_copies[o].start()

    @pl.when(date == last - 4)
    def _():
        for by in (2, 3):
            pl.semaphore_signal(ready, inc=1, device_id={"date": date_after(by)}, device_id_type=MESH)

    loads = []
    for n, (src, dst) in enumerate(((f_hbm, f_vm), (map_hbm, map_ref), (mask_hbm, mask_ref))):
        copy = pltpu.make_async_copy(src, dst, lsem.at[n])
        copy.start()
        loads.append(copy)

    @pl.when((date == late) | (date == late + 1))
    def _():
        pl.semaphore_wait(ready, 1)
        date_copies[0].start()

    pl.when(date == late)(date_copies[1].start)

    eye = (lax.broadcasted_iota(jnp.int32, (cols, cols), 0)
           == lax.broadcasted_iota(jnp.int32, (cols, cols), 1)).astype(jnp.bfloat16)
    for o in range(SHIFTS):
        padf[o, :PAD, :] = jnp.zeros((PAD, yc), jnp.float32)
        padf[o, PAD + cols:, :] = jnp.zeros((PAD, yc), jnp.float32)
    loads[0].wait()
    full = f_vm[...].astype(jnp.float32)
    fr_ref[0] = full
    for kb in range(1, DISP // 8):
        fr_ref[kb] = pltpu.roll(full, cols - 8 * kb, 1)
    for copy in loads[1:]:
        copy.wait()

    start = col * cols - EDGE - cols * col_count // 2
    row_ids = lax.broadcasted_iota(jnp.int32, (8, yc), 1) // chans
    sub_ids = lax.broadcasted_iota(jnp.int32, (8, yc), 0)
    for n, o in enumerate((1, 0, 2)):
        h0, h1, h2 = map_ref[o, 0, 0], map_ref[o, 0, 1], map_ref[o, 0, 2]
        base = h0 + h1 * start
        least = base + jnp.minimum(h1 * (reach - 1), 0) + jnp.minimum(h2 * (rows - 1), 0)
        shift = least >> 12
        first_row = PAD - EDGE + shift
        scale = mask_ref[0, o].astype(jnp.float32) * (GROUPS / chans)
        unit = scale / 4096.0
        numer = (base - shift * 4096) + h1 * sub_ids + h2 * row_ids
        ramp = numer.astype(jnp.float32) * unit
        step = (h1 * 8).astype(jnp.float32) * unit
        date_copies[o].wait_recv()
        padf[o, PAD:PAD + cols, :] = lax.dot_general(
            eye, got[o], (((1,), (1,)), ((), ())), preferred_element_type=jnp.float32)
        for i in range(reach // 8):
            e = ramp + step * float(i) if i else ramp
            w0 = jnp.maximum(scale - e, 0.0)
            w2 = jnp.maximum(e - scale, 0.0)
            w1 = scale - w0 - w2
            term = (w0 * padf[o, pl.ds(first_row + 8 * i, 8), :]
                    + w1 * padf[o, pl.ds(first_row + 8 * i + 1, 8), :]
                    + w2 * padf[o, pl.ds(first_row + 8 * i + 2, 8), :])
            if n == 0:
                part[pl.ds(8 * i, 8), :] = term
            else:
                part[pl.ds(8 * i, 8), :] += term

    col_copies = []
    for n, (src, size, dst, by) in enumerate((
            (0, EDGE, right1, -1),
            (reach - TAIL, TAIL, left2, 2),
            (0, reach, left1, 1))):
        copy = pltpu.make_async_remote_copy(
            src_ref=part.at[pl.ds(src, size)], dst_ref=dst, send_sem=csend.at[n], recv_sem=crecv.at[n],
            device_id={"col": col_of(by)}, device_id_type=MESH)
        sends = (col + by >= 0) & (col + by < col_count)
        comes = (col - by >= 0) & (col - by < col_count)
        pl.when(sends)(copy.start)
        col_copies.append((copy, sends, comes))

    at1 = DMAX - EDGE
    at0 = at1 + cols
    at_r = at0 + cols
    wt[pl.ds(at0, cols + EDGE), :] = part[:cols + EDGE, :]
    for copy, _, comes in col_copies:
        pl.when(comes)(copy.wait_recv)
    over = TAIL - at1

    @pl.when(col > 1)
    def _():
        wt[:at1, :] = left2[:at1, :]
        wt[at1:at1 + over, :] = left2[at1:, :] + left1[:over, :]

    @pl.when(col == 1)
    def _():
        wt[:at1, :] = jnp.zeros((at1, yc), jnp.float32)
        wt[at1:at1 + over, :] = left1[:over, :]

    @pl.when(col > 0)
    def _():
        wt[at1 + over:at0, :] = left1[over:cols, :]
        wt[at0:at0 + 2 * EDGE, :] += left1[cols:, :]

    @pl.when(col == 0)
    def _():
        wt[:at0, :] = jnp.zeros((at0, yc), jnp.float32)

    @pl.when(col < col_count - 1)
    def _():
        wt[at_r:at_r + EDGE, :] += right1[...]

    for copy in date_copies:
        copy.wait_send()
    for copy, sends, _ in col_copies:
        pl.when(sends)(copy.wait_send)


def correlate_kernel(disp_ref, wt_ref, fr_ref, o_hbm, w_ref, buf, even, odd, sem):
    total_groups, disps, cols = o_hbm.shape
    chans = w_ref.shape[0] // total_groups
    batch = even.shape[0] // chans
    batches = total_groups // batch
    lanes = lax.broadcasted_iota(jnp.int32, (8, cols), 1)

    def skew(into, which):
        for n in range(batch * chans):
            wide = jnp.broadcast_to(w_ref[pl.ds(which * batch * chans + n, 1), :], (8, w_ref.shape[1]))
            skewed = pltpu.roll(wide, 0, 1, stride=1, stride_axis=0)
            into[n, 0] = skewed[:, :cols]
            into[n, 1] = skewed[:, cols:]

    def score(held, which):
        for q in range(batch):
            g = which * batch + q
            lows = [held[q * chans + c, 0] for c in range(chans)]
            highs = [held[q * chans + c, 1] for c in range(chans)]
            blocks = []
            for kb in range(disps // 8):
                total = None
                for c in range(chans):
                    tile = highs[c] if kb == 0 else jnp.where(lanes >= cols - 8 * kb, lows[c], highs[c])
                    term = jnp.broadcast_to(fr_ref[kb, pl.ds(g * chans + c, 1), :], (8, cols)) * tile
                    total = term if total is None else total + term
                blocks.append(pltpu.roll(total, 8 * kb, 1) if kb else total)
                if len(blocks) == 2:
                    buf[g, pl.ds(8 * (kb - 1), 16), :] = jnp.concatenate(blocks, axis=0).astype(buf.dtype)
                    blocks = []
            pltpu.make_async_copy(buf.at[g], o_hbm.at[g], sem).start()

    for n in range((cols + DISP) // cols):
        w_ref[:, pl.ds(n * cols, cols)] = wt_ref[pl.ds(DMAX - disp_ref[0] + n * cols, cols), :].T
    skew(even, 0)

    for n in range(batches // 2):
        skew(odd, 2 * n + 1)
        score(even, 2 * n)
        if n + 1 < batches // 2:
            skew(even, 2 * n + 2)
        score(odd, 2 * n + 1)

    pltpu.make_async_copy(buf, o_hbm, sem).wait()


def shards(features, column_map, pair_mask, disp_start):
    rows, chans, cols = features.shape[1:]
    yc = rows * chans
    tile = features.reshape(yc, cols)
    dates, col_count = lax.axis_size("date"), lax.axis_size("col")
    anywhere = pl.BlockSpec(memory_space=pl.ANY)
    vmem = pl.BlockSpec(memory_space=pltpu.VMEM)
    reach = cols + 2 * EDGE
    warped, rolled = pl.pallas_call(
        functools.partial(exchange_kernel, dates, col_count, rows),
        out_shape=(pltpu.VMEM((DMAX + 2 * cols, yc), jnp.float32),
                   pltpu.VMEM((DISP // 8, yc, cols), jnp.float32)),
        in_specs=[anywhere] * 3,
        out_specs=(vmem, vmem),
        scratch_shapes=[
            pltpu.VMEM((yc, cols), jnp.bfloat16),
            pltpu.SMEM((SHIFTS, 1, 3), jnp.int32),
            pltpu.SMEM((1, SHIFTS), jnp.int32),
            pltpu.VMEM((SHIFTS, yc, cols), jnp.bfloat16),
            pltpu.VMEM((SHIFTS, cols + 2 * PAD, yc), jnp.float32),
            pltpu.VMEM((reach, yc), jnp.float32),
            pltpu.VMEM((reach, yc), jnp.float32),
            pltpu.VMEM((TAIL, yc), jnp.float32),
            pltpu.VMEM((EDGE, yc), jnp.float32),
            pltpu.SemaphoreType.DMA((3,)),
            pltpu.SemaphoreType.DMA((SHIFTS,)),
            pltpu.SemaphoreType.DMA((SHIFTS,)),
            pltpu.SemaphoreType.DMA((3,)),
            pltpu.SemaphoreType.DMA((3,)),
            pltpu.SemaphoreType.REGULAR,
        ],
        compiler_params=pltpu.CompilerParams(collective_id=0, has_side_effects=True),
        name="exchange",
    )(jnp.transpose(column_map, (1, 0, 2)), pair_mask, tile)
    warped = pltpu.with_memory_space_constraint(warped, pltpu.VMEM)
    rolled = pltpu.with_memory_space_constraint(rolled, pltpu.VMEM)
    cost = pl.pallas_call(
        correlate_kernel,
        out_shape=jax.ShapeDtypeStruct((rows * GROUPS, DISP, cols), jnp.bfloat16),
        in_specs=[pl.BlockSpec(memory_space=pltpu.SMEM), vmem, vmem],
        out_specs=anywhere,
        scratch_shapes=[
            pltpu.VMEM((yc, cols + DISP), jnp.float32),
            pltpu.VMEM((rows * GROUPS, DISP, cols), jnp.bfloat16),
            pltpu.VMEM((BATCH * chans // GROUPS, 2, 8, cols), jnp.float32),
            pltpu.VMEM((BATCH * chans // GROUPS, 2, 8, cols), jnp.float32),
            pltpu.SemaphoreType.DMA,
        ],
        name="correlate",
    )(disp_start, warped, rolled)
    return cost.reshape(1, rows, GROUPS, DISP, cols)


def solution(mesh):
    return jax.shard_map(
        shards,
        mesh=mesh,
        in_specs=(P("date", None, None, "col"), P("date", None, None), P("date", None), P("date")),
        out_specs=P("date", None, None, None, "col"),
        check_vma=False,
    )
```

```python
import functools

import jax
import jax.numpy as jnp
from jax import lax
from jax.experimental import pallas as pl
from jax.experimental.pallas import tpu as pltpu
from jax.sharding import PartitionSpec as P

GROUPS = 8
DISP = 128
SHIFTS = 3
EDGE = 16
PAD = 32
TAIL = 48
DMAX = 32
BATCH = 4
MESH = pl.DeviceIdType.MESH


def exchange_kernel(dates, col_count, rows, map_hbm, mask_hbm, f_hbm, wt, fr_ref,
                    f_vm, map_ref, mask_ref, got, padf, part, left1, left2, right1,
                    lsem, dsend, drecv, csend, crecv, ready):
    date = lax.axis_index("date")
    col = lax.axis_index("col")
    yc, cols = f_hbm.shape
    chans = yc // rows
    reach = cols + 2 * EDGE

    def date_before(by):
        return jnp.where(date < by, date - by + dates, date - by)

    def date_after(by):
        return jnp.where(date + by >= dates, date + by - dates, date + by)

    def col_of(by):
        return jnp.clip(col + by, 0, col_count - 1)

    late = dates - SHIFTS
    last = dates - 1
    barrier = pltpu.get_barrier_semaphore()
    near = jnp.where(col > 0, 1, 0) + jnp.where(col < col_count - 1, 1, 0) + jnp.where(col < col_count - 2, 1, 0)
    date_copies = []
    for o in range(SHIFTS):
        date_copies.append(pltpu.make_async_remote_copy(
            src_ref=f_hbm, dst_ref=got.at[o], send_sem=dsend.at[o], recv_sem=drecv.at[o],
            device_id={"date": date_after(o + 1)}, device_id_type=MESH))

    @pl.when(date >= late)
    def _():
        for here, direct, beside in ((date == late, 1, 0), (date == late + 1, 2, 1), (date == last, 3, 1)):
            @pl.when(here)
            def _():
                pl.semaphore_wait(barrier, direct + beside * near)
        pl.when(date == last)(date_copies[0].start)
        pl.when(date < last)(date_copies[2].start)
        pl.when(date == late + 1)(date_copies[1].start)

    for o in (1, 2, 3):
        @pl.when(date < late + o)
        def _():
            pl.semaphore_signal(barrier, inc=1, device_id={"date": date_before(o)}, device_id_type=MESH)

    @pl.when(date == last)
    def _():
        pl.semaphore_signal(barrier, inc=1, device_id={"date": date_before(4)}, device_id_type=MESH)

    back = jnp.where(date >= late, date - late + 1, 2)
    for by in (-2, -1, 1):
        @pl.when((col + by >= 0) & (col + by < col_count))
        def _():
            pl.semaphore_signal(barrier, inc=1, device_id={"date": date_before(back), "col": col_of(by)},
                                device_id_type=MESH)

    @pl.when(date < late)
    def _():
        for here, direct, beside in ((date < last - 4, 3, 1), (date == last - 4, 4, 0), (date == last - 3, 3, 3)):
            @pl.when(here)
            def _():
                pl.semaphore_wait(barrier, direct + beside * near)
        for o in (2, 0, 1):
            date_copies[o].start()

    @pl.when(date == last - 4)
    def _():
        for by in (2, 3):
            pl.semaphore_signal(ready, inc=1, device_id={"date": date_after(by)}, device_id_type=MESH)

    loads = []
    for n, (src, dst) in enumerate(((f_hbm, f_vm), (map_hbm, map_ref), (mask_hbm, mask_ref))):
        copy = pltpu.make_async_copy(src, dst, lsem.at[n])
        copy.start()
        loads.append(copy)

    @pl.when((date == late) | (date == late + 1))
    def _():
        pl.semaphore_wait(ready, 1)
        date_copies[0].start()

    pl.when(date == late)(date_copies[1].start)

    eye = (lax.broadcasted_iota(jnp.int32, (cols, cols), 0)
           == lax.broadcasted_iota(jnp.int32, (cols, cols), 1)).astype(jnp.bfloat16)
    for o in range(SHIFTS):
        padf[o, :PAD, :] = jnp.zeros((PAD, yc), jnp.float32)
        padf[o, PAD + cols:, :] = jnp.zeros((PAD, yc), jnp.float32)
    loads[0].wait()
    pl.when(date == last)(date_copies[2].start)
    full = f_vm[...].astype(jnp.float32)
    fr_ref[0] = full
    for kb in range(1, DISP // 8):
        fr_ref[kb] = pltpu.roll(full, cols - 8 * kb, 1)
    pl.when(date == last)(date_copies[1].start)
    for copy in loads[1:]:
        copy.wait()

    start = col * cols - EDGE - cols * col_count // 2
    row_ids = lax.broadcasted_iota(jnp.int32, (8, yc), 1) // chans
    sub_ids = lax.broadcasted_iota(jnp.int32, (8, yc), 0)
    for n, o in enumerate((1, 0, 2)):
        h0, h1, h2 = map_ref[o, 0, 0], map_ref[o, 0, 1], map_ref[o, 0, 2]
        base = h0 + h1 * start
        least = base + jnp.minimum(h1 * (reach - 1), 0) + jnp.minimum(h2 * (rows - 1), 0)
        shift = least >> 12
        first_row = PAD - EDGE + shift
        scale = mask_ref[0, o].astype(jnp.float32) * (GROUPS / chans)
        unit = scale / 4096.0
        numer = (base - shift * 4096) + h1 * sub_ids + h2 * row_ids
        ramp = numer.astype(jnp.float32) * unit
        step = (h1 * 8).astype(jnp.float32) * unit
        date_copies[o].wait_recv()
        padf[o, PAD:PAD + cols, :] = lax.dot_general(
            eye, got[o], (((1,), (1,)), ((), ())), preferred_element_type=jnp.float32)
        for i in range(reach // 8):
            e = ramp + step * float(i) if i else ramp
            w0 = jnp.maximum(scale - e, 0.0)
            w2 = jnp.maximum(e - scale, 0.0)
            w1 = scale - w0 - w2
            term = (w0 * padf[o, pl.ds(first_row + 8 * i, 8), :]
                    + w1 * padf[o, pl.ds(first_row + 8 * i + 1, 8), :]
                    + w2 * padf[o, pl.ds(first_row + 8 * i + 2, 8), :])
            if n == 0:
                part[pl.ds(8 * i, 8), :] = term
            else:
                part[pl.ds(8 * i, 8), :] += term

    col_copies = []
    for n, (src, size, dst, by) in enumerate((
            (0, EDGE, right1, -1),
            (reach - TAIL, TAIL, left2, 2),
            (0, reach, left1, 1))):
        copy = pltpu.make_async_remote_copy(
            src_ref=part.at[pl.ds(src, size)], dst_ref=dst, send_sem=csend.at[n], recv_sem=crecv.at[n],
            device_id={"col": col_of(by)}, device_id_type=MESH)
        sends = (col + by >= 0) & (col + by < col_count)
        comes = (col - by >= 0) & (col - by < col_count)
        pl.when(sends)(copy.start)
        col_copies.append((copy, sends, comes))

    at1 = DMAX - EDGE
    at0 = at1 + cols
    at_r = at0 + cols
    wt[pl.ds(at0, cols + EDGE), :] = part[:cols + EDGE, :]
    for copy, _, comes in col_copies:
        pl.when(comes)(copy.wait_recv)
    over = TAIL - at1

    @pl.when(col > 1)
    def _():
        wt[:at1, :] = left2[:at1, :]
        wt[at1:at1 + over, :] = left2[at1:, :] + left1[:over, :]

    @pl.when(col == 1)
    def _():
        wt[:at1, :] = jnp.zeros((at1, yc), jnp.float32)
        wt[at1:at1 + over, :] = left1[:over, :]

    @pl.when(col > 0)
    def _():
        wt[at1 + over:at0, :] = left1[over:cols, :]
        wt[at0:at0 + 2 * EDGE, :] += left1[cols:, :]

    @pl.when(col == 0)
    def _():
        wt[:at0, :] = jnp.zeros((at0, yc), jnp.float32)

    @pl.when(col < col_count - 1)
    def _():
        wt[at_r:at_r + EDGE, :] += right1[...]

    for copy in date_copies:
        copy.wait_send()
    for copy, sends, _ in col_copies:
        pl.when(sends)(copy.wait_send)


def correlate_kernel(disp_ref, wt_ref, fr_ref, o_hbm, w_ref, buf, even, odd, sem):
    total_groups, disps, cols = o_hbm.shape
    chans = w_ref.shape[0] // total_groups
    batch = even.shape[0] // chans
    batches = total_groups // batch
    lanes = lax.broadcasted_iota(jnp.int32, (8, cols), 1)

    def skew(into, which):
        for n in range(batch * chans):
            wide = jnp.broadcast_to(w_ref[pl.ds(which * batch * chans + n, 1), :], (8, w_ref.shape[1]))
            skewed = pltpu.roll(wide, 0, 1, stride=1, stride_axis=0)
            into[n, 0] = skewed[:, :cols]
            into[n, 1] = skewed[:, cols:]

    def score(held, which):
        for q in range(batch):
            g = which * batch + q
            lows = [held[q * chans + c, 0] for c in range(chans)]
            highs = [held[q * chans + c, 1] for c in range(chans)]
            blocks = []
            for kb in range(disps // 8):
                total = None
                for c in range(chans):
                    tile = highs[c] if kb == 0 else jnp.where(lanes >= cols - 8 * kb, lows[c], highs[c])
                    term = jnp.broadcast_to(fr_ref[kb, pl.ds(g * chans + c, 1), :], (8, cols)) * tile
                    total = term if total is None else total + term
                blocks.append(pltpu.roll(total, 8 * kb, 1) if kb else total)
                if len(blocks) == 2:
                    buf[g, pl.ds(8 * (kb - 1), 16), :] = jnp.concatenate(blocks, axis=0).astype(buf.dtype)
                    blocks = []
            pltpu.make_async_copy(buf.at[g], o_hbm.at[g], sem).start()

    for n in range((cols + DISP) // cols):
        w_ref[:, pl.ds(n * cols, cols)] = wt_ref[pl.ds(DMAX - disp_ref[0] + n * cols, cols), :].T
    skew(even, 0)

    for n in range(batches // 2):
        skew(odd, 2 * n + 1)
        score(even, 2 * n)
        if n + 1 < batches // 2:
            skew(even, 2 * n + 2)
        score(odd, 2 * n + 1)

    pltpu.make_async_copy(buf, o_hbm, sem).wait()


def shards(features, column_map, pair_mask, disp_start):
    rows, chans, cols = features.shape[1:]
    yc = rows * chans
    tile = features.reshape(yc, cols)
    dates, col_count = lax.axis_size("date"), lax.axis_size("col")
    anywhere = pl.BlockSpec(memory_space=pl.ANY)
    vmem = pl.BlockSpec(memory_space=pltpu.VMEM)
    reach = cols + 2 * EDGE
    warped, rolled = pl.pallas_call(
        functools.partial(exchange_kernel, dates, col_count, rows),
        out_shape=(pltpu.VMEM((DMAX + 2 * cols, yc), jnp.float32),
                   pltpu.VMEM((DISP // 8, yc, cols), jnp.float32)),
        in_specs=[anywhere] * 3,
        out_specs=(vmem, vmem),
        scratch_shapes=[
            pltpu.VMEM((yc, cols), jnp.bfloat16),
            pltpu.SMEM((SHIFTS, 1, 3), jnp.int32),
            pltpu.SMEM((1, SHIFTS), jnp.int32),
            pltpu.VMEM((SHIFTS, yc, cols), jnp.bfloat16),
            pltpu.VMEM((SHIFTS, cols + 2 * PAD, yc), jnp.float32),
            pltpu.VMEM((reach, yc), jnp.float32),
            pltpu.VMEM((reach, yc), jnp.float32),
            pltpu.VMEM((TAIL, yc), jnp.float32),
            pltpu.VMEM((EDGE, yc), jnp.float32),
            pltpu.SemaphoreType.DMA((3,)),
            pltpu.SemaphoreType.DMA((SHIFTS,)),
            pltpu.SemaphoreType.DMA((SHIFTS,)),
            pltpu.SemaphoreType.DMA((3,)),
            pltpu.SemaphoreType.DMA((3,)),
            pltpu.SemaphoreType.REGULAR,
        ],
        compiler_params=pltpu.CompilerParams(collective_id=0, has_side_effects=True),
        name="exchange",
    )(jnp.transpose(column_map, (1, 0, 2)), pair_mask, tile)
    warped = pltpu.with_memory_space_constraint(warped, pltpu.VMEM)
    rolled = pltpu.with_memory_space_constraint(rolled, pltpu.VMEM)
    cost = pl.pallas_call(
        correlate_kernel,
        out_shape=jax.ShapeDtypeStruct((rows * GROUPS, DISP, cols), jnp.bfloat16),
        in_specs=[pl.BlockSpec(memory_space=pltpu.SMEM), vmem, vmem],
        out_specs=anywhere,
        scratch_shapes=[
            pltpu.VMEM((yc, cols + DISP), jnp.float32),
            pltpu.VMEM((rows * GROUPS, DISP, cols), jnp.bfloat16),
            pltpu.VMEM((BATCH * chans // GROUPS, 2, 8, cols), jnp.float32),
            pltpu.VMEM((BATCH * chans // GROUPS, 2, 8, cols), jnp.float32),
            pltpu.SemaphoreType.DMA,
        ],
        name="correlate",
    )(disp_start, warped, rolled)
    return cost.reshape(1, rows, GROUPS, DISP, cols)


def solution(mesh):
    return jax.shard_map(
        shards,
        mesh=mesh,
        in_specs=(P("date", None, None, "col"), P("date", None, None), P("date", None), P("date")),
        out_specs=P("date", None, None, None, "col"),
        check_vma=False,
    )
```

```python
import functools

import jax
import jax.numpy as jnp
from jax import lax
from jax.experimental import pallas as pl
from jax.experimental.pallas import tpu as pltpu
from jax.sharding import PartitionSpec as P

GROUPS = 8
DISP = 128
SHIFTS = 3
EDGE = 16
PAD = 32
TAIL = 48
DMAX = 32
BATCH = 4
MESH = pl.DeviceIdType.MESH


def exchange_kernel(dates, col_count, rows, map_hbm, mask_hbm, f_hbm, wt, fr_ref,
                    f_vm, map_ref, mask_ref, got, padf, part, left1, left2, right1,
                    lsem, dsend, drecv, csend, crecv, ready):
    date = lax.axis_index("date")
    col = lax.axis_index("col")
    yc, cols = f_hbm.shape
    chans = yc // rows
    reach = cols + 2 * EDGE

    def date_before(by):
        return jnp.where(date < by, date - by + dates, date - by)

    def date_after(by):
        return jnp.where(date + by >= dates, date + by - dates, date + by)

    def col_of(by):
        return jnp.clip(col + by, 0, col_count - 1)

    late = dates - SHIFTS
    last = dates - 1
    barrier = pltpu.get_barrier_semaphore()
    near = jnp.where(col > 0, 1, 0) + jnp.where(col < col_count - 1, 1, 0) + jnp.where(col < col_count - 2, 1, 0)
    date_copies = []
    for o in range(SHIFTS):
        date_copies.append(pltpu.make_async_remote_copy(
            src_ref=f_hbm, dst_ref=got.at[o], send_sem=dsend.at[o], recv_sem=drecv.at[o],
            device_id={"date": date_after(o + 1)}, device_id_type=MESH))

    @pl.when(date >= late)
    def _():
        for here, direct, beside in ((date == late, 1, 0), (date == late + 1, 2, 1), (date == last, 3, 1)):
            @pl.when(here)
            def _():
                pl.semaphore_wait(barrier, direct + beside * near)
        pl.when(date == last)(date_copies[0].start)
        pl.when(date < last)(date_copies[2].start)
        pl.when(date == late + 1)(date_copies[1].start)

    for o in (1, 2, 3):
        @pl.when(date < late + o)
        def _():
            pl.semaphore_signal(barrier, inc=1, device_id={"date": date_before(o)}, device_id_type=MESH)

    @pl.when(date == last)
    def _():
        pl.semaphore_signal(barrier, inc=1, device_id={"date": date_before(4)}, device_id_type=MESH)

    back = jnp.where(date >= late, date - late + 1, 2)
    for by in (-2, -1, 1):
        @pl.when((col + by >= 0) & (col + by < col_count))
        def _():
            pl.semaphore_signal(barrier, inc=1, device_id={"date": date_before(back), "col": col_of(by)},
                                device_id_type=MESH)

    @pl.when(date < late)
    def _():
        for here, direct, beside in ((date < last - 4, 3, 1), (date == last - 4, 4, 0), (date == last - 3, 3, 3)):
            @pl.when(here)
            def _():
                pl.semaphore_wait(barrier, direct + beside * near)
        for o in (2, 0, 1):
            date_copies[o].start()

    @pl.when(date == last - 4)
    def _():
        for by in (2, 3):
            pl.semaphore_signal(ready, inc=1, device_id={"date": date_after(by)}, device_id_type=MESH)

    loads = []
    for n, (src, dst) in enumerate(((f_hbm, f_vm), (map_hbm, map_ref), (mask_hbm, mask_ref))):
        copy = pltpu.make_async_copy(src, dst, lsem.at[n])
        copy.start()
        loads.append(copy)

    @pl.when((date == late) | (date == late + 1))
    def _():
        pl.semaphore_wait(ready, 1)
        date_copies[0].start()

    pl.when(date == late)(date_copies[1].start)

    eye = (lax.broadcasted_iota(jnp.int32, (cols, cols), 0)
           == lax.broadcasted_iota(jnp.int32, (cols, cols), 1)).astype(jnp.bfloat16)
    for o in range(SHIFTS):
        padf[o, :PAD, :] = jnp.zeros((PAD, yc), jnp.float32)
        padf[o, PAD + cols:, :] = jnp.zeros((PAD, yc), jnp.float32)
    loads[0].wait()
    pl.when(date == last)(date_copies[2].start)
    full = f_vm[...].astype(jnp.float32)
    fr_ref[0] = full
    for kb in range(1, DISP // 8):
        fr_ref[kb] = pltpu.roll(full, cols - 8 * kb, 1)
    pl.when(date == last)(date_copies[1].start)
    for copy in loads[1:]:
        copy.wait()

    start = col * cols - EDGE - cols * col_count // 2
    row_ids = lax.broadcasted_iota(jnp.int32, (8, yc), 1) // chans
    sub_ids = lax.broadcasted_iota(jnp.int32, (8, yc), 0)
    for n, o in enumerate((1, 0, 2)):
        h0, h1, h2 = map_ref[o, 0, 0], map_ref[o, 0, 1], map_ref[o, 0, 2]
        base = h0 + h1 * start
        least = base + jnp.minimum(h1 * (reach - 1), 0) + jnp.minimum(h2 * (rows - 1), 0)
        shift = least >> 12
        first_row = PAD - EDGE + shift
        scale = mask_ref[0, o].astype(jnp.float32) * (GROUPS / chans)
        unit = scale / 4096.0
        numer = (base - shift * 4096) + h1 * sub_ids + h2 * row_ids
        ramp = numer.astype(jnp.float32) * unit
        step = (h1 * 8).astype(jnp.float32) * unit
        date_copies[o].wait_recv()
        padf[o, PAD:PAD + cols, :] = lax.dot_general(
            eye, got[o], (((1,), (1,)), ((), ())), preferred_element_type=jnp.float32)
        for i in range(reach // 8):
            e = ramp + step * float(i) if i else ramp
            w0 = jnp.maximum(scale - e, 0.0)
            w2 = jnp.maximum(e - scale, 0.0)
            w1 = scale - w0 - w2
            term = (w0 * padf[o, pl.ds(first_row + 8 * i, 8), :]
                    + w1 * padf[o, pl.ds(first_row + 8 * i + 1, 8), :]
                    + w2 * padf[o, pl.ds(first_row + 8 * i + 2, 8), :])
            if n == 0:
                part[pl.ds(8 * i, 8), :] = term
            else:
                part[pl.ds(8 * i, 8), :] += term

    col_copies = []
    for n, (src, size, dst, by) in enumerate((
            (0, EDGE, right1, -1),
            (reach - TAIL, TAIL, left2, 2),
            (0, reach, left1, 1))):
        copy = pltpu.make_async_remote_copy(
            src_ref=part.at[pl.ds(src, size)], dst_ref=dst, send_sem=csend.at[n], recv_sem=crecv.at[n],
            device_id={"col": col_of(by)}, device_id_type=MESH)
        sends = (col + by >= 0) & (col + by < col_count)
        comes = (col - by >= 0) & (col - by < col_count)
        col_copies.append((copy, sends, comes))
    even = lax.rem(col, 2) == 0
    for n, when in ((0, col >= 0), (2, even), (1, col >= 0), (2, jnp.logical_not(even))):
        pl.when(col_copies[n][1] & when)(col_copies[n][0].start)

    at1 = DMAX - EDGE
    at0 = at1 + cols
    at_r = at0 + cols
    wt[pl.ds(at0, cols + EDGE), :] = part[:cols + EDGE, :]
    for copy, _, comes in col_copies:
        pl.when(comes)(copy.wait_recv)
    over = TAIL - at1

    @pl.when(col > 1)
    def _():
        wt[:at1, :] = left2[:at1, :]
        wt[at1:at1 + over, :] = left2[at1:, :] + left1[:over, :]

    @pl.when(col == 1)
    def _():
        wt[:at1, :] = jnp.zeros((at1, yc), jnp.float32)
        wt[at1:at1 + over, :] = left1[:over, :]

    @pl.when(col > 0)
    def _():
        wt[at1 + over:at0, :] = left1[over:cols, :]
        wt[at0:at0 + 2 * EDGE, :] += left1[cols:, :]

    @pl.when(col == 0)
    def _():
        wt[:at0, :] = jnp.zeros((at0, yc), jnp.float32)

    @pl.when(col < col_count - 1)
    def _():
        wt[at_r:at_r + EDGE, :] += right1[...]

    for copy in date_copies:
        copy.wait_send()
    for copy, sends, _ in col_copies:
        pl.when(sends)(copy.wait_send)


def correlate_kernel(disp_ref, wt_ref, fr_ref, o_hbm, w_ref, buf, even, odd, sem):
    total_groups, disps, cols = o_hbm.shape
    chans = w_ref.shape[0] // total_groups
    batch = even.shape[0] // chans
    batches = total_groups // batch
    lanes = lax.broadcasted_iota(jnp.int32, (8, cols), 1)

    def skew(into, which):
        for n in range(batch * chans):
            wide = jnp.broadcast_to(w_ref[pl.ds(which * batch * chans + n, 1), :], (8, w_ref.shape[1]))
            skewed = pltpu.roll(wide, 0, 1, stride=1, stride_axis=0)
            into[n, 0] = skewed[:, :cols]
            into[n, 1] = skewed[:, cols:]

    def score(held, which):
        for q in range(batch):
            g = which * batch + q
            lows = [held[q * chans + c, 0] for c in range(chans)]
            highs = [held[q * chans + c, 1] for c in range(chans)]
            blocks = []
            for kb in range(disps // 8):
                total = None
                for c in range(chans):
                    tile = highs[c] if kb == 0 else jnp.where(lanes >= cols - 8 * kb, lows[c], highs[c])
                    term = jnp.broadcast_to(fr_ref[kb, pl.ds(g * chans + c, 1), :], (8, cols)) * tile
                    total = term if total is None else total + term
                blocks.append(pltpu.roll(total, 8 * kb, 1) if kb else total)
                if len(blocks) == 2:
                    buf[g, pl.ds(8 * (kb - 1), 16), :] = jnp.concatenate(blocks, axis=0).astype(buf.dtype)
                    blocks = []
            pltpu.make_async_copy(buf.at[g], o_hbm.at[g], sem).start()

    for n in range((cols + DISP) // cols):
        w_ref[:, pl.ds(n * cols, cols)] = wt_ref[pl.ds(DMAX - disp_ref[0] + n * cols, cols), :].T
    skew(even, 0)

    for n in range(batches // 2):
        skew(odd, 2 * n + 1)
        score(even, 2 * n)
        if n + 1 < batches // 2:
            skew(even, 2 * n + 2)
        score(odd, 2 * n + 1)

    pltpu.make_async_copy(buf, o_hbm, sem).wait()


def shards(features, column_map, pair_mask, disp_start):
    rows, chans, cols = features.shape[1:]
    yc = rows * chans
    tile = features.reshape(yc, cols)
    dates, col_count = lax.axis_size("date"), lax.axis_size("col")
    anywhere = pl.BlockSpec(memory_space=pl.ANY)
    vmem = pl.BlockSpec(memory_space=pltpu.VMEM)
    reach = cols + 2 * EDGE
    warped, rolled = pl.pallas_call(
        functools.partial(exchange_kernel, dates, col_count, rows),
        out_shape=(pltpu.VMEM((DMAX + 2 * cols, yc), jnp.float32),
                   pltpu.VMEM((DISP // 8, yc, cols), jnp.float32)),
        in_specs=[anywhere] * 3,
        out_specs=(vmem, vmem),
        scratch_shapes=[
            pltpu.VMEM((yc, cols), jnp.bfloat16),
            pltpu.SMEM((SHIFTS, 1, 3), jnp.int32),
            pltpu.SMEM((1, SHIFTS), jnp.int32),
            pltpu.VMEM((SHIFTS, yc, cols), jnp.bfloat16),
            pltpu.VMEM((SHIFTS, cols + 2 * PAD, yc), jnp.float32),
            pltpu.VMEM((reach, yc), jnp.float32),
            pltpu.VMEM((reach, yc), jnp.float32),
            pltpu.VMEM((TAIL, yc), jnp.float32),
            pltpu.VMEM((EDGE, yc), jnp.float32),
            pltpu.SemaphoreType.DMA((3,)),
            pltpu.SemaphoreType.DMA((SHIFTS,)),
            pltpu.SemaphoreType.DMA((SHIFTS,)),
            pltpu.SemaphoreType.DMA((3,)),
            pltpu.SemaphoreType.DMA((3,)),
            pltpu.SemaphoreType.REGULAR,
        ],
        compiler_params=pltpu.CompilerParams(collective_id=0, has_side_effects=True),
        name="exchange",
    )(jnp.transpose(column_map, (1, 0, 2)), pair_mask, tile)
    warped = pltpu.with_memory_space_constraint(warped, pltpu.VMEM)
    rolled = pltpu.with_memory_space_constraint(rolled, pltpu.VMEM)
    cost = pl.pallas_call(
        correlate_kernel,
        out_shape=jax.ShapeDtypeStruct((rows * GROUPS, DISP, cols), jnp.bfloat16),
        in_specs=[pl.BlockSpec(memory_space=pltpu.SMEM), vmem, vmem],
        out_specs=anywhere,
        scratch_shapes=[
            pltpu.VMEM((yc, cols + DISP), jnp.float32),
            pltpu.VMEM((rows * GROUPS, DISP, cols), jnp.bfloat16),
            pltpu.VMEM((BATCH * chans // GROUPS, 2, 8, cols), jnp.float32),
            pltpu.VMEM((BATCH * chans // GROUPS, 2, 8, cols), jnp.float32),
            pltpu.SemaphoreType.DMA,
        ],
        name="correlate",
    )(disp_start, warped, rolled)
    return cost.reshape(1, rows, GROUPS, DISP, cols)


def solution(mesh):
    return jax.shard_map(
        shards,
        mesh=mesh,
        in_specs=(P("date", None, None, "col"), P("date", None, None), P("date", None), P("date")),
        out_specs=P("date", None, None, None, "col"),
        check_vma=False,
    )
```

```python
import functools

import jax
import jax.numpy as jnp
from jax import lax
from jax.experimental import pallas as pl
from jax.experimental.pallas import tpu as pltpu
from jax.sharding import PartitionSpec as P

GROUPS = 8
DISP = 128
SHIFTS = 3
EDGE = 16
PAD = 32
TAIL = 48
DMAX = 32
BATCH = 4
MESH = pl.DeviceIdType.MESH


def exchange_kernel(dates, col_count, rows, map_hbm, mask_hbm, f_hbm, wt, fr_ref,
                    f_vm, map_ref, mask_ref, got, padf, part, left1, left2, right1,
                    lsem, dsend, drecv, csend, crecv, ready):
    date = lax.axis_index("date")
    col = lax.axis_index("col")
    yc, cols = f_hbm.shape
    chans = yc // rows
    reach = cols + 2 * EDGE

    def date_before(by):
        return jnp.where(date < by, date - by + dates, date - by)

    def date_after(by):
        return jnp.where(date + by >= dates, date + by - dates, date + by)

    def col_of(by):
        return jnp.clip(col + by, 0, col_count - 1)

    late = dates - SHIFTS
    last = dates - 1
    barrier = pltpu.get_barrier_semaphore()
    near = jnp.where(col > 0, 1, 0) + jnp.where(col < col_count - 1, 1, 0) + jnp.where(col < col_count - 2, 1, 0)
    date_copies = []
    for o in range(SHIFTS):
        date_copies.append(pltpu.make_async_remote_copy(
            src_ref=f_hbm, dst_ref=got.at[o], send_sem=dsend.at[o], recv_sem=drecv.at[o],
            device_id={"date": date_after(o + 1)}, device_id_type=MESH))

    @pl.when(date == late)
    def _():
        pl.semaphore_wait(barrier, 1)
        date_copies[2].start()

    @pl.when(date > late)
    def _():
        pl.semaphore_wait(barrier, jnp.where(date == last, 3, 2) + near)
        pl.when(date == last)(date_copies[0].start)

        @pl.when(date < last)
        def _():
            date_copies[2].start()
            date_copies[1].start()

    for o in (1, 2, 3):
        @pl.when(date < late + o)
        def _():
            pl.semaphore_signal(barrier, inc=1, device_id={"date": date_before(o)}, device_id_type=MESH)

    @pl.when(date == last)
    def _():
        pl.semaphore_signal(barrier, inc=1, device_id={"date": date_before(4)}, device_id_type=MESH)

    back = jnp.where(date >= late, date - late + 1, 2)
    for by in (-2, -1, 1):
        @pl.when((col + by >= 0) & (col + by < col_count))
        def _():
            pl.semaphore_signal(barrier, inc=1, device_id={"date": date_before(back), "col": col_of(by)},
                                device_id_type=MESH)

    @pl.when(date < late)
    def _():
        for here, direct, beside in ((date < last - 4, 3, 1), (date == last - 4, 4, 0), (date == last - 3, 3, 3)):
            @pl.when(here)
            def _():
                pl.semaphore_wait(barrier, direct + beside * near)
        for o in (2, 0, 1):
            date_copies[o].start()

    @pl.when(date == last - 4)
    def _():
        for by in (2, 3):
            pl.semaphore_signal(ready, inc=1, device_id={"date": date_after(by)}, device_id_type=MESH)

    loads = []
    for n, (src, dst) in enumerate(((f_hbm, f_vm), (map_hbm, map_ref), (mask_hbm, mask_ref))):
        copy = pltpu.make_async_copy(src, dst, lsem.at[n])
        copy.start()
        loads.append(copy)

    @pl.when((date == late) | (date == late + 1))
    def _():
        pl.semaphore_wait(ready, 1)
        date_copies[0].start()

    pl.when(date == late)(date_copies[1].start)

    eye = (lax.broadcasted_iota(jnp.int32, (cols, cols), 0)
           == lax.broadcasted_iota(jnp.int32, (cols, cols), 1)).astype(jnp.bfloat16)
    for o in range(SHIFTS):
        padf[o, :PAD, :] = jnp.zeros((PAD, yc), jnp.float32)
        padf[o, PAD + cols:, :] = jnp.zeros((PAD, yc), jnp.float32)
    pl.when(date == last)(date_copies[2].start)
    loads[0].wait()
    full = f_vm[...].astype(jnp.float32)
    fr_ref[0] = full
    for kb in range(1, DISP // 8):
        fr_ref[kb] = pltpu.roll(full, cols - 8 * kb, 1)
    pl.when(date == last)(date_copies[1].start)
    for copy in loads[1:]:
        copy.wait()

    start = col * cols - EDGE - cols * col_count // 2
    row_ids = lax.broadcasted_iota(jnp.int32, (8, yc), 1) // chans
    sub_ids = lax.broadcasted_iota(jnp.int32, (8, yc), 0)
    for n, o in enumerate((1, 0, 2)):
        h0, h1, h2 = map_ref[o, 0, 0], map_ref[o, 0, 1], map_ref[o, 0, 2]
        base = h0 + h1 * start
        least = base + jnp.minimum(h1 * (reach - 1), 0) + jnp.minimum(h2 * (rows - 1), 0)
        shift = least >> 12
        first_row = PAD - EDGE + shift
        scale = mask_ref[0, o].astype(jnp.float32) * (GROUPS / chans)
        unit = scale / 4096.0
        numer = (base - shift * 4096) + h1 * sub_ids + h2 * row_ids
        ramp = numer.astype(jnp.float32) * unit
        step = (h1 * 8).astype(jnp.float32) * unit
        date_copies[o].wait_recv()
        padf[o, PAD:PAD + cols, :] = lax.dot_general(
            eye, got[o], (((1,), (1,)), ((), ())), preferred_element_type=jnp.float32)
        for i in range(reach // 8):
            e = ramp + step * float(i) if i else ramp
            w0 = jnp.maximum(scale - e, 0.0)
            w2 = jnp.maximum(e - scale, 0.0)
            w1 = scale - w0 - w2
            term = (w0 * padf[o, pl.ds(first_row + 8 * i, 8), :]
                    + w1 * padf[o, pl.ds(first_row + 8 * i + 1, 8), :]
                    + w2 * padf[o, pl.ds(first_row + 8 * i + 2, 8), :])
            if n == 0:
                part[pl.ds(8 * i, 8), :] = term
            else:
                part[pl.ds(8 * i, 8), :] += term

    col_copies = []
    for n, (src, size, dst, by) in enumerate((
            (0, EDGE, right1, -1),
            (reach - TAIL, TAIL, left2, 2),
            (0, reach, left1, 1))):
        copy = pltpu.make_async_remote_copy(
            src_ref=part.at[pl.ds(src, size)], dst_ref=dst, send_sem=csend.at[n], recv_sem=crecv.at[n],
            device_id={"col": col_of(by)}, device_id_type=MESH)
        sends = (col + by >= 0) & (col + by < col_count)
        comes = (col - by >= 0) & (col - by < col_count)
        pl.when(sends)(copy.start)
        col_copies.append((copy, sends, comes))

    at1 = DMAX - EDGE
    at0 = at1 + cols
    at_r = at0 + cols
    wt[pl.ds(at0, cols + EDGE), :] = part[:cols + EDGE, :]
    for copy, _, comes in col_copies:
        pl.when(comes)(copy.wait_recv)
    over = TAIL - at1

    @pl.when(col > 1)
    def _():
        wt[:at1, :] = left2[:at1, :]
        wt[at1:at1 + over, :] = left2[at1:, :] + left1[:over, :]

    @pl.when(col == 1)
    def _():
        wt[:at1, :] = jnp.zeros((at1, yc), jnp.float32)
        wt[at1:at1 + over, :] = left1[:over, :]

    @pl.when(col > 0)
    def _():
        wt[at1 + over:at0, :] = left1[over:cols, :]
        wt[at0:at0 + 2 * EDGE, :] += left1[cols:, :]

    @pl.when(col == 0)
    def _():
        wt[:at0, :] = jnp.zeros((at0, yc), jnp.float32)

    @pl.when(col < col_count - 1)
    def _():
        wt[at_r:at_r + EDGE, :] += right1[...]

    for copy in date_copies:
        copy.wait_send()
    for copy, sends, _ in col_copies:
        pl.when(sends)(copy.wait_send)


def correlate_kernel(disp_ref, wt_ref, fr_ref, o_hbm, w_ref, buf, even, odd, sem):
    total_groups, disps, cols = o_hbm.shape
    chans = w_ref.shape[0] // total_groups
    batch = even.shape[0] // chans
    batches = total_groups // batch
    lanes = lax.broadcasted_iota(jnp.int32, (8, cols), 1)

    def skew(into, which):
        for n in range(batch * chans):
            wide = jnp.broadcast_to(w_ref[pl.ds(which * batch * chans + n, 1), :], (8, w_ref.shape[1]))
            skewed = pltpu.roll(wide, 0, 1, stride=1, stride_axis=0)
            into[n, 0] = skewed[:, :cols]
            into[n, 1] = skewed[:, cols:]

    def score(held, which):
        for q in range(batch):
            g = which * batch + q
            lows = [held[q * chans + c, 0] for c in range(chans)]
            highs = [held[q * chans + c, 1] for c in range(chans)]
            blocks = []
            for kb in range(disps // 8):
                total = None
                for c in range(chans):
                    tile = highs[c] if kb == 0 else jnp.where(lanes >= cols - 8 * kb, lows[c], highs[c])
                    term = jnp.broadcast_to(fr_ref[kb, pl.ds(g * chans + c, 1), :], (8, cols)) * tile
                    total = term if total is None else total + term
                blocks.append(pltpu.roll(total, 8 * kb, 1) if kb else total)
                if len(blocks) == 2:
                    buf[g, pl.ds(8 * (kb - 1), 16), :] = jnp.concatenate(blocks, axis=0).astype(buf.dtype)
                    blocks = []
            pltpu.make_async_copy(buf.at[g], o_hbm.at[g], sem).start()

    for n in range((cols + DISP) // cols):
        w_ref[:, pl.ds(n * cols, cols)] = wt_ref[pl.ds(DMAX - disp_ref[0] + n * cols, cols), :].T
    skew(even, 0)

    for n in range(batches // 2):
        skew(odd, 2 * n + 1)
        score(even, 2 * n)
        if n + 1 < batches // 2:
            skew(even, 2 * n + 2)
        score(odd, 2 * n + 1)

    pltpu.make_async_copy(buf, o_hbm, sem).wait()


def shards(features, column_map, pair_mask, disp_start):
    rows, chans, cols = features.shape[1:]
    yc = rows * chans
    tile = features.reshape(yc, cols)
    dates, col_count = lax.axis_size("date"), lax.axis_size("col")
    anywhere = pl.BlockSpec(memory_space=pl.ANY)
    vmem = pl.BlockSpec(memory_space=pltpu.VMEM)
    reach = cols + 2 * EDGE
    warped, rolled = pl.pallas_call(
        functools.partial(exchange_kernel, dates, col_count, rows),
        out_shape=(pltpu.VMEM((DMAX + 2 * cols, yc), jnp.float32),
                   pltpu.VMEM((DISP // 8, yc, cols), jnp.float32)),
        in_specs=[anywhere] * 3,
        out_specs=(vmem, vmem),
        scratch_shapes=[
            pltpu.VMEM((yc, cols), jnp.bfloat16),
            pltpu.SMEM((SHIFTS, 1, 3), jnp.int32),
            pltpu.SMEM((1, SHIFTS), jnp.int32),
            pltpu.VMEM((SHIFTS, yc, cols), jnp.bfloat16),
            pltpu.VMEM((SHIFTS, cols + 2 * PAD, yc), jnp.float32),
            pltpu.VMEM((reach, yc), jnp.float32),
            pltpu.VMEM((reach, yc), jnp.float32),
            pltpu.VMEM((TAIL, yc), jnp.float32),
            pltpu.VMEM((EDGE, yc), jnp.float32),
            pltpu.SemaphoreType.DMA((3,)),
            pltpu.SemaphoreType.DMA((SHIFTS,)),
            pltpu.SemaphoreType.DMA((SHIFTS,)),
            pltpu.SemaphoreType.DMA((3,)),
            pltpu.SemaphoreType.DMA((3,)),
            pltpu.SemaphoreType.REGULAR,
        ],
        compiler_params=pltpu.CompilerParams(collective_id=0, has_side_effects=True),
        name="exchange",
    )(jnp.transpose(column_map, (1, 0, 2)), pair_mask, tile)
    warped = pltpu.with_memory_space_constraint(warped, pltpu.VMEM)
    rolled = pltpu.with_memory_space_constraint(rolled, pltpu.VMEM)
    cost = pl.pallas_call(
        correlate_kernel,
        out_shape=jax.ShapeDtypeStruct((rows * GROUPS, DISP, cols), jnp.bfloat16),
        in_specs=[pl.BlockSpec(memory_space=pltpu.SMEM), vmem, vmem],
        out_specs=anywhere,
        scratch_shapes=[
            pltpu.VMEM((yc, cols + DISP), jnp.float32),
            pltpu.VMEM((rows * GROUPS, DISP, cols), jnp.bfloat16),
            pltpu.VMEM((BATCH * chans // GROUPS, 2, 8, cols), jnp.float32),
            pltpu.VMEM((BATCH * chans // GROUPS, 2, 8, cols), jnp.float32),
            pltpu.SemaphoreType.DMA,
        ],
        name="correlate",
    )(disp_start, warped, rolled)
    return cost.reshape(1, rows, GROUPS, DISP, cols)


def solution(mesh):
    return jax.shard_map(
        shards,
        mesh=mesh,
        in_specs=(P("date", None, None, "col"), P("date", None, None), P("date", None), P("date")),
        out_specs=P("date", None, None, None, "col"),
        check_vma=False,
    )
```
